512 devices in a mesh: section: 4 (over y_hi), tile: 64 (over x, z, core), rep: 2 (over y_lo).
Axes of the slice: x: 4, y: 8 (y_hi: 4, y_lo: 2; y = y_hi * 2 + y_lo), z: 8, core: 2. Of those that a mesh axis runs over, the one named last changes fastest.
Arguments:
- phase_shift: float32 [4, 64, 384, 384], P('section', 'tile'), may hold values from -3.140625 to 3.140625
- absorption: float32 [4, 64, 384, 384], P('section', 'tile'), may hold values from 0 to 0.5
- probe_wave: float32 [2, 256, 256], replicated, may hold values from -6 to 6
- positions: int32 [64, 2, 1, 2], P('tile', 'rep'), may hold values from 0 to 384
- counts: int32 [64, 2, 1, 256, 256], P('tile', 'rep'), may hold values from 0 to 7
Outputs:
- phase_gradient: float32 [4, 64, 384, 384], P('section', 'tile', 'rep')
- absorption_gradient: float32 [4, 64, 384, 384], P('section', 'tile', 'rep')
The draws below stay inside these ranges and needn't reach their ends.
All inputs are finite; a program needn't handle non-finite values.
Results may differ from the reference program's by a relative error of at most 0.00027.
Values sent between devices are 32-bit elements; how exact they have to be, the bound alone decides.
A program may use at most 64 MiB of HBM per device.

```python
import math
import jax
import jax.numpy as jnp
from jax import lax

FR = 256
TL = 384
HALO = 128
F_DEV = 1
SLICES = 4
N_TILE = 64
N_REP = 2


def touch_ends(drawn, own_key, least, top_value):
    spot = [jax.random.randint(jax.random.fold_in(own_key, axis), (), 0, length) for axis, length in enumerate(drawn.shape)]
    main_axis = drawn.shape.index(max(drawn.shape))
    neighbour = spot[:main_axis] + [(spot[main_axis] + 1) % drawn.shape[main_axis]] + spot[main_axis + 1:]
    return drawn.at[tuple(spot)].set(least).at[tuple(neighbour)].set(top_value)


def steps_of(key, extent, pieces, least, high):
    factor_of, own = 1.0, jax.random.fold_in(key, 6)
    for dim, parts in pieces:
        draws = jnp.exp(jax.random.uniform(jax.random.fold_in(own, dim), (parts,), jnp.float32, least / len(pieces), high / len(pieces)))
        factor_of = factor_of * jnp.repeat(draws, extent[dim] // parts).reshape([-1 if axis == dim else 1 for axis in range(len(extent))])
    return factor_of


def scatter_about(stream_key, shape, width, reach, kind=jnp.bfloat16):
    array = jax.random.normal(stream_key, shape, jnp.float32) * width
    return jnp.minimum(jnp.maximum(array, -reach), reach).astype(kind)


def setup_inputs(seed: int = 0) -> dict:
    splits = jax.random.split(jax.random.key(seed), 6)
    phase_shift = jnp.clip(jax.random.uniform(splits[0], (SLICES, N_TILE, TL, TL), jnp.float32, -3.140625, 3.140625), -3.140625, 3.140625)
    absorption = jnp.clip(0.5 * jax.random.uniform(splits[1], (SLICES, N_TILE, TL, TL), jnp.float32) ** steps_of(splits[1], (SLICES, N_TILE, TL, TL), ((0, 4), (1, 64)), -0.2, 0.2), 0.0, 0.5)
    probe_wave = scatter_about(splits[2], (2, FR, FR), 1.0, 6.0, jnp.float32)
    positions = touch_ends(jax.random.randint(splits[3], (N_TILE, N_REP, F_DEV, 2), 0, TL + 2 * HALO - FR + 1), jax.random.fold_in(splits[3], 1), 0, TL + 2 * HALO - FR).astype(jnp.int32)
    counts = touch_ends(jax.random.randint(splits[4], (N_TILE, N_REP, F_DEV, FR, FR), 0, 8), jax.random.fold_in(splits[4], 1), 0, 7).astype(jnp.int32)
    return {"phase_shift": phase_shift, "absorption": absorption, "probe_wave": probe_wave, "positions": positions, "counts": counts}


dead_time = 0.1
background = 0.1
loss_weight = 0.1
fresnel = 0.5

def kernel_angles(length):
    indices = jnp.arange(length, dtype=jnp.int32)
    shifted = jnp.where(indices < length // 2, indices, indices - length).astype(jnp.float32)
    return math.pi * fresnel * shifted * shifted / length

def likelihood_seed(far_re, far_im, observed):
    intensity = far_re * far_re + far_im * far_im
    shifted_total = intensity + background
    denominator = 1.0 + dead_time * shifted_total
    model_rate = shifted_total / denominator
    slope_term = loss_weight * (1.0 - observed / model_rate) / (denominator * denominator)
    return (2.0 * slope_term * far_re, 2.0 * slope_term * far_im)

def reference(phase_shift, absorption, probe_wave, positions, counts):
    grid_side = math.isqrt(N_TILE)
    span = grid_side * TL
    padded_side = span + 2 * HALO

    def assemble(field_in):
        blocks = field_in.reshape(SLICES, grid_side, grid_side, TL, TL).transpose(0, 1, 3, 2, 4)
        blocks = blocks.reshape(SLICES, span, span)
        return jnp.pad(blocks, ((0, 0), (HALO, HALO), (HALO, HALO)))
    full_phase = assemble(phase_shift)
    full_absorb = assemble(absorption)
    damping = jnp.exp(-full_absorb)
    trans_re = damping * jnp.cos(full_phase)
    trans_im = damping * jnp.sin(full_phase)
    angles = kernel_angles(FR)
    kernel_line = lax.complex(jnp.cos(angles), jnp.sin(angles))
    kernel_plane = kernel_line[:, None] * kernel_line[None, :]
    probe_field = lax.complex(probe_wave[0], probe_wave[1])
    tile_ids = jnp.repeat(jnp.arange(N_TILE, dtype=jnp.int32), N_REP * F_DEV)
    flat_positions = positions.reshape(N_TILE * N_REP * F_DEV, 2).astype(jnp.int32)
    row_starts = (tile_ids // grid_side * TL + flat_positions[:, 0]).astype(jnp.int32)
    col_starts = (tile_ids % grid_side * TL + flat_positions[:, 1]).astype(jnp.int32)
    observed_all = counts.reshape(N_TILE * N_REP * F_DEV, FR, FR).astype(jnp.float32)

    def visit(totals, item):
        row_at, col_at, observed = item
        phase_totals = list(totals[0])
        absorb_totals = list(totals[1])
        wave_now = probe_field
        objects = []
        exit_waves = []
        for slice_no in range(SLICES):
            window_re = lax.dynamic_slice(trans_re[slice_no], (row_at, col_at), (FR, FR))
            window_im = lax.dynamic_slice(trans_im[slice_no], (row_at, col_at), (FR, FR))
            object_field = lax.complex(window_re, window_im)
            exit_wave = object_field * wave_now
            objects.append(object_field)
            exit_waves.append(exit_wave)
            if slice_no < SLICES - 1:
                wave_now = jnp.fft.ifft2(jnp.fft.fft2(exit_wave) * kernel_plane)
            else:
                wave_now = jnp.fft.fft2(exit_wave, norm='ortho')
        seed_re, seed_im = likelihood_seed(jnp.real(wave_now), jnp.imag(wave_now), observed)
        grad_wave = lax.complex(seed_re, seed_im)
        for slice_no in reversed(range(SLICES)):
            if slice_no < SLICES - 1:
                back_wave = jnp.fft.ifft2(jnp.fft.fft2(grad_wave) * jnp.conj(kernel_plane))
            else:
                back_wave = jnp.fft.ifft2(grad_wave, norm='ortho')
            product = jnp.conj(back_wave) * exit_waves[slice_no]
            phase_term = -jnp.imag(product)
            absorb_term = -jnp.real(product)
            current = lax.dynamic_slice(phase_totals[slice_no], (row_at, col_at), (FR, FR))
            phase_totals[slice_no] = lax.dynamic_update_slice(phase_totals[slice_no], current + phase_term, (row_at, col_at))
            current = lax.dynamic_slice(absorb_totals[slice_no], (row_at, col_at), (FR, FR))
            absorb_totals[slice_no] = lax.dynamic_update_slice(absorb_totals[slice_no], current + absorb_term, (row_at, col_at))
            grad_wave = jnp.conj(objects[slice_no]) * back_wave
        return ((tuple(phase_totals), tuple(absorb_totals)), None)
    empty_planes = tuple((jnp.zeros((padded_side, padded_side), jnp.float32) for slice_no in range(SLICES)))
    totals, unused = lax.scan(visit, (empty_planes, empty_planes), (row_starts, col_starts, observed_all))

    def disassemble(planes):
        inner = jnp.stack(planes)[:, HALO:HALO + span, HALO:HALO + span]
        inner = inner.reshape(SLICES, grid_side, TL, grid_side, TL).transpose(0, 1, 3, 2, 4)
        return inner.reshape(SLICES, N_TILE, TL, TL)
    return (disassemble(totals[0]), disassemble(totals[1]))
```

```python
import math

import jax
import jax.numpy as jnp
from jax import lax
from jax.sharding import PartitionSpec as P

HALO = 128


dead_time = 0.1
background = 0.1
loss_weight = 0.1
fresnel = 0.5
highest = lax.Precision.HIGHEST


def from_behind(value, axis, by):
    peers = lax.axis_size(axis)
    pairs = [(i, i + by) for i in range(peers) if 0 <= i + by < peers]
    return lax.ppermute(value, axis, pairs)


def left_product(matrix, frames):
    return jnp.einsum(
        "mk,bkn->bmn", matrix, frames, precision=highest, preferred_element_type=jnp.float32
    )


def right_product(frames, matrix):
    return jnp.einsum(
        "bmk,kn->bmn", frames, matrix, precision=highest, preferred_element_type=jnp.float32
    )


def sandwich(table_re, table_im, wave_re, wave_im):
    first_re = left_product(table_re, wave_re) - left_product(table_im, wave_im)
    first_im = left_product(table_re, wave_im) + left_product(table_im, wave_re)
    out_re = right_product(first_re, table_re) - right_product(first_im, table_im)
    out_im = right_product(first_re, table_im) + right_product(first_im, table_re)
    return (out_re, out_im)


def dft_tables(length):
    indices = jnp.arange(length, dtype=jnp.int32)
    product = indices[:, None] * indices[None, :] % length
    angles = product.astype(jnp.float32) * (2.0 * math.pi / length)
    cosine_table = jnp.cos(angles)
    sine_table = jnp.sin(angles)
    shifted = jnp.where(indices < length // 2, indices, indices - length).astype(jnp.float32)
    kernel = math.pi * fresnel * shifted * shifted / length

    def spread(weights):
        first_part = jnp.dot(cosine_table * weights[None, :], cosine_table, precision=highest)
        second_part = jnp.dot(sine_table * weights[None, :], sine_table, precision=highest)
        return (first_part + second_part) / length

    near_table = (spread(jnp.cos(kernel)), spread(jnp.sin(kernel)))
    norm_scale = 1.0 / math.sqrt(length)
    far_table = (cosine_table * norm_scale, -sine_table * norm_scale)
    return (near_table, far_table)


def block_tables(table_re, table_im):
    left = jnp.stack([jnp.stack([table_re, -table_im]), jnp.stack([table_im, table_re])])
    right = jnp.stack([jnp.stack([table_re, table_im]), jnp.stack([-table_im, table_re])])
    return (left, right)


def stacked_sandwich(pair, wave_re, wave_im):
    left, right = pair
    wave = jnp.stack([wave_re, wave_im])
    first = jnp.einsum("abmk,bkn->amn", left, wave, precision=highest, preferred_element_type=jnp.float32)
    out = jnp.einsum("bmk,bakn->amn", first, right, precision=highest, preferred_element_type=jnp.float32)
    return (out[0], out[1])


def likelihood_seed(far_re, far_im, observed):
    intensity = far_re * far_re + far_im * far_im
    shifted_total = intensity + background
    denominator = 1.0 + dead_time * shifted_total
    model_rate = shifted_total / denominator
    slope_term = loss_weight * (1.0 - observed / model_rate) / (denominator * denominator)
    return (2.0 * slope_term * far_re, 2.0 * slope_term * far_im)


def shards(phase_shift, absorption, probe_wave, positions, counts):
    slices_here = phase_shift.shape[0]
    tile_width = phase_shift.shape[2]
    frame_width = probe_wave.shape[1]
    sections = lax.axis_size("section")
    tile_count = lax.axis_size("tile")
    grid_side = math.isqrt(tile_count)
    margin = HALO
    extent = tile_width + 2 * margin
    section_index = lax.axis_index("section")
    column = lax.axis_index("tile") % grid_side
    has_left = (column > 0).astype(jnp.float32)
    has_right = (column < grid_side - 1).astype(jnp.float32)
    own_block = jnp.stack([phase_shift[:, 0], absorption[:, 0]])

    def fetch_rim(rim_strip, offset):
        return from_behind(rim_strip, "tile", offset)

    upper_rim = fetch_rim(own_block[:, :, tile_width - margin :, :], grid_side)
    lower_rim = fetch_rim(own_block[:, :, :margin, :], -grid_side)
    tall_block = jnp.concatenate([upper_rim, own_block, lower_rim], axis=2)
    left_rim = fetch_rim(tall_block[:, :, :, tile_width - margin :], 1) * has_left
    right_rim = fetch_rim(tall_block[:, :, :, :margin], -1) * has_right
    extended = jnp.concatenate([left_rim, tall_block, right_rim], axis=3)
    slices_total = sections * slices_here
    corner = positions[0, 0, 0]
    window = lax.dynamic_slice(
        extended, (0, 0, corner[0], corner[1]), (2, slices_here, frame_width, frame_width)
    )
    damping = jnp.exp(-window[1])
    own_objects = jnp.stack([damping * jnp.cos(window[0]), damping * jnp.sin(window[0])], axis=1)
    all_objects = lax.all_gather(own_objects, "section", axis=0, tiled=True)
    near_table, far_table = dft_tables(frame_width)
    near_pair = block_tables(*near_table)
    far_pair = block_tables(*far_table)
    near_back = block_tables(near_table[0], -near_table[1])
    far_back = block_tables(far_table[0], -far_table[1])
    observed = counts[0, 0, 0].astype(jnp.float32)
    wave_re, wave_im = probe_wave[0], probe_wave[1]
    exits = []
    for slice_no in range(slices_total):
        object_re = all_objects[slice_no, 0]
        object_im = all_objects[slice_no, 1]
        exit_re = object_re * wave_re - object_im * wave_im
        exit_im = object_re * wave_im + object_im * wave_re
        exits.append((exit_re, exit_im))
        pair = near_pair if slice_no < slices_total - 1 else far_pair
        wave_re, wave_im = stacked_sandwich(pair, exit_re, exit_im)
    grad_re, grad_im = likelihood_seed(wave_re, wave_im, observed)
    terms = []
    for slice_no in reversed(range(slices_total)):
        pair = near_back if slice_no < slices_total - 1 else far_back
        back_re, back_im = stacked_sandwich(pair, grad_re, grad_im)
        exit_re, exit_im = exits[slice_no]
        phase_term = back_im * exit_re - back_re * exit_im
        absorb_term = -(back_re * exit_re + back_im * exit_im)
        terms.append(jnp.stack([phase_term, absorb_term]))
        if slice_no > 0:
            object_re = all_objects[slice_no, 0]
            object_im = all_objects[slice_no, 1]
            grad_re = object_re * back_re + object_im * back_im
            grad_im = object_re * back_im - object_im * back_re
    terms = jnp.stack(terms[::-1], axis=1)
    own_terms = lax.dynamic_slice_in_dim(terms, section_index * slices_here, slices_here, axis=1)
    grad_extended = jnp.zeros((2, slices_here, extent, extent), jnp.float32)
    grad_extended = lax.dynamic_update_slice(grad_extended, own_terms, (0, 0, corner[0], corner[1]))

    def give_back(rim_strip, offset):
        return from_behind(rim_strip, "tile", offset)

    from_below = give_back(grad_extended[:, :, :margin, :], -grid_side)
    from_above = give_back(grad_extended[:, :, tile_width + margin :, :], grid_side)
    body_rows = grad_extended[:, :, margin : margin + tile_width, :]
    body_rows = body_rows.at[:, :, :margin].add(from_above)
    body_rows = body_rows.at[:, :, tile_width - margin :].add(from_below)
    from_right = give_back(body_rows[..., :margin], -1) * has_right
    from_left = give_back(body_rows[..., tile_width + margin :], 1) * has_left
    middle = body_rows[..., margin : margin + tile_width]
    middle = middle.at[..., :margin].add(from_left)
    middle = middle.at[..., tile_width - margin :].add(from_right)
    shares = lax.psum_scatter(middle, "rep", scatter_dimension=2, tiled=True)
    return (shares[0][:, None], shares[1][:, None])


def solution(mesh):
    in_specs = (
        P("section", "tile", None, None),
        P("section", "tile", None, None),
        P(),
        P("tile", "rep", None, None),
        P("tile", "rep", None, None, None),
    )
    out_specs = (P("section", "tile", "rep", None), P("section", "tile", "rep", None))
    return jax.shard_map(shards, mesh=mesh, in_specs=in_specs, out_specs=out_specs, check_vma=False)
```

```python
import math

import jax
import jax.numpy as jnp
from jax import lax
from jax.sharding import PartitionSpec as P

HALO = 128


dead_time = 0.1
background = 0.1
loss_weight = 0.1
fresnel = 0.5
highest = lax.Precision.HIGHEST


def from_behind(value, axis, by):
    peers = lax.axis_size(axis)
    pairs = [(i, i + by) for i in range(peers) if 0 <= i + by < peers]
    return lax.ppermute(value, axis, pairs)


def left_product(matrix, frames):
    return jnp.einsum(
        "mk,bkn->bmn", matrix, frames, precision=highest, preferred_element_type=jnp.float32
    )


def right_product(frames, matrix):
    return jnp.einsum(
        "bmk,kn->bmn", frames, matrix, precision=highest, preferred_element_type=jnp.float32
    )


def sandwich(table_re, table_im, wave_re, wave_im):
    first_re = left_product(table_re, wave_re) - left_product(table_im, wave_im)
    first_im = left_product(table_re, wave_im) + left_product(table_im, wave_re)
    out_re = right_product(first_re, table_re) - right_product(first_im, table_im)
    out_im = right_product(first_re, table_im) + right_product(first_im, table_re)
    return (out_re, out_im)


def dft_tables(length):
    indices = jnp.arange(length, dtype=jnp.int32)
    product = indices[:, None] * indices[None, :] % length
    angles = product.astype(jnp.float32) * (2.0 * math.pi / length)
    cosine_table = jnp.cos(angles)
    sine_table = jnp.sin(angles)
    shifted = jnp.where(indices < length // 2, indices, indices - length).astype(jnp.float32)
    kernel = math.pi * fresnel * shifted * shifted / length

    def spread(weights):
        first_part = jnp.dot(cosine_table * weights[None, :], cosine_table, precision=highest)
        second_part = jnp.dot(sine_table * weights[None, :], sine_table, precision=highest)
        return (first_part + second_part) / length

    near_table = (spread(jnp.cos(kernel)), spread(jnp.sin(kernel)))
    norm_scale = 1.0 / math.sqrt(length)
    far_table = (cosine_table * norm_scale, -sine_table * norm_scale)
    return (near_table, far_table)


def block_tables(table_re, table_im):
    left = jnp.stack([jnp.stack([table_re, -table_im]), jnp.stack([table_im, table_re])])
    right = jnp.stack([jnp.stack([table_re, table_im]), jnp.stack([-table_im, table_re])])
    return (left, right)


def stacked_sandwich(pair, wave_re, wave_im):
    left, right = pair
    wave = jnp.stack([wave_re, wave_im])
    first = jnp.einsum("abmk,bkn->amn", left, wave, precision=highest, preferred_element_type=jnp.float32)
    out = jnp.einsum("bmk,bakn->amn", first, right, precision=highest, preferred_element_type=jnp.float32)
    return (out[0], out[1])


def likelihood_seed(far_re, far_im, observed):
    intensity = far_re * far_re + far_im * far_im
    shifted_total = intensity + background
    denominator = 1.0 + dead_time * shifted_total
    model_rate = shifted_total / denominator
    slope_term = loss_weight * (1.0 - observed / model_rate) / (denominator * denominator)
    return (2.0 * slope_term * far_re, 2.0 * slope_term * far_im)


def shards(phase_shift, absorption, probe_wave, positions, counts):
    slices_here = phase_shift.shape[0]
    tile_width = phase_shift.shape[2]
    frame_width = probe_wave.shape[1]
    sections = lax.axis_size("section")
    tile_count = lax.axis_size("tile")
    grid_side = math.isqrt(tile_count)
    margin = HALO
    extent = tile_width + 2 * margin
    section_index = lax.axis_index("section")
    column = lax.axis_index("tile") % grid_side
    has_left = (column > 0).astype(jnp.float32)
    has_right = (column < grid_side - 1).astype(jnp.float32)
    own_block = jnp.stack([phase_shift[:, 0], absorption[:, 0]])

    low, high = tile_width - margin, margin

    def fetch(strip, offset, keep=None):
        got = from_behind(strip, "tile", offset)
        return got if keep is None else got * keep

    above = fetch(own_block[:, :, low:, :], grid_side)
    below = fetch(own_block[:, :, :high, :], -grid_side)
    to_left = fetch(own_block[:, :, :, low:], 1, has_left)
    to_right = fetch(own_block[:, :, :, :high], -1, has_right)
    above_left = fetch(own_block[:, :, low:, low:], grid_side + 1, has_left)
    above_right = fetch(own_block[:, :, low:, :high], grid_side - 1, has_right)
    below_left = fetch(own_block[:, :, :high, low:], 1 - grid_side, has_left)
    below_right = fetch(own_block[:, :, :high, :high], -1 - grid_side, has_right)
    extended = jnp.concatenate(
        [
            jnp.concatenate([above_left, above, above_right], axis=3),
            jnp.concatenate([to_left, own_block, to_right], axis=3),
            jnp.concatenate([below_left, below, below_right], axis=3),
        ],
        axis=2,
    )
    slices_total = sections * slices_here
    corner = positions[0, 0, 0]
    window = lax.dynamic_slice(
        extended, (0, 0, corner[0], corner[1]), (2, slices_here, frame_width, frame_width)
    )
    damping = jnp.exp(-window[1])
    own_objects = jnp.stack([damping * jnp.cos(window[0]), damping * jnp.sin(window[0])], axis=1)
    all_objects = lax.all_gather(own_objects, "section", axis=0, tiled=True)
    near_table, far_table = dft_tables(frame_width)
    near_pair = block_tables(*near_table)
    far_pair = block_tables(*far_table)
    near_back = block_tables(near_table[0], -near_table[1])
    far_back = block_tables(far_table[0], -far_table[1])
    observed = counts[0, 0, 0].astype(jnp.float32)
    wave_re, wave_im = probe_wave[0], probe_wave[1]
    exits = []
    for slice_no in range(slices_total):
        object_re = all_objects[slice_no, 0]
        object_im = all_objects[slice_no, 1]
        exit_re = object_re * wave_re - object_im * wave_im
        exit_im = object_re * wave_im + object_im * wave_re
        exits.append((exit_re, exit_im))
        pair = near_pair if slice_no < slices_total - 1 else far_pair
        wave_re, wave_im = stacked_sandwich(pair, exit_re, exit_im)
    grad_re, grad_im = likelihood_seed(wave_re, wave_im, observed)
    terms = []
    for slice_no in reversed(range(slices_total)):
        pair = near_back if slice_no < slices_total - 1 else far_back
        back_re, back_im = stacked_sandwich(pair, grad_re, grad_im)
        exit_re, exit_im = exits[slice_no]
        phase_term = back_im * exit_re - back_re * exit_im
        absorb_term = -(back_re * exit_re + back_im * exit_im)
        terms.append(jnp.stack([phase_term, absorb_term]))
        if slice_no > 0:
            object_re = all_objects[slice_no, 0]
            object_im = all_objects[slice_no, 1]
            grad_re = object_re * back_re + object_im * back_im
            grad_im = object_re * back_im - object_im * back_re
    terms = jnp.stack(terms[::-1], axis=1)
    own_terms = lax.dynamic_slice_in_dim(terms, section_index * slices_here, slices_here, axis=1)
    reach = extent - frame_width
    padded_terms = jnp.pad(own_terms, ((0, 0), (0, 0), (reach, reach), (reach, reach)))
    grad_extended = lax.dynamic_slice(
        padded_terms, (0, 0, reach - corner[0], reach - corner[1]), (2, slices_here, extent, extent)
    )
    inner = slice(margin, margin + tile_width)
    top, bottom = slice(0, margin), slice(margin + tile_width, extent)

    def give_back(rows, cols, offset, keep=None):
        got = from_behind(grad_extended[:, :, rows, cols], "tile", offset)
        return got if keep is None else got * keep

    middle = grad_extended[:, :, inner, inner]
    middle = middle.at[:, :, low:, :].add(give_back(top, inner, -grid_side))
    middle = middle.at[:, :, :high, :].add(give_back(bottom, inner, grid_side))
    middle = middle.at[:, :, :, low:].add(give_back(inner, top, -1, has_right))
    middle = middle.at[:, :, :, :high].add(give_back(inner, bottom, 1, has_left))
    middle = middle.at[:, :, low:, low:].add(give_back(top, top, -1 - grid_side, has_right))
    middle = middle.at[:, :, low:, :high].add(give_back(top, bottom, 1 - grid_side, has_left))
    middle = middle.at[:, :, :high, low:].add(give_back(bottom, top, grid_side - 1, has_right))
    middle = middle.at[:, :, :high, :high].add(give_back(bottom, bottom, grid_side + 1, has_left))
    half = tile_width // 2
    rep_index = lax.axis_index("rep")
    kept = lax.dynamic_slice_in_dim(middle, rep_index * half, half, axis=2)
    sent = lax.dynamic_slice_in_dim(middle, (1 - rep_index) * half, half, axis=2)
    shares = kept + lax.ppermute(sent, "rep", [(0, 1), (1, 0)])
    return (shares[0][:, None], shares[1][:, None])


def solution(mesh):
    in_specs = (
        P("section", "tile", None, None),
        P("section", "tile", None, None),
        P(),
        P("tile", "rep", None, None),
        P("tile", "rep", None, None, None),
    )
    out_specs = (P("section", "tile", "rep", None), P("section", "tile", "rep", None))
    return jax.shard_map(shards, mesh=mesh, in_specs=in_specs, out_specs=out_specs, check_vma=False)
```

```python
import math

import jax
import jax.numpy as jnp
from jax import lax
from jax.sharding import PartitionSpec as P

HALO = 128


dead_time = 0.1
background = 0.1
loss_weight = 0.1
fresnel = 0.5
highest = lax.Precision.HIGHEST


def from_behind(value, axis, by):
    peers = lax.axis_size(axis)
    pairs = [(i, i + by) for i in range(peers) if 0 <= i + by < peers]
    return lax.ppermute(value, axis, pairs)


def left_product(matrix, frames):
    return jnp.einsum(
        "mk,bkn->bmn", matrix, frames, precision=highest, preferred_element_type=jnp.float32
    )


def right_product(frames, matrix):
    return jnp.einsum(
        "bmk,kn->bmn", frames, matrix, precision=highest, preferred_element_type=jnp.float32
    )


def sandwich(table_re, table_im, wave_re, wave_im):
    first_re = left_product(table_re, wave_re) - left_product(table_im, wave_im)
    first_im = left_product(table_re, wave_im) + left_product(table_im, wave_re)
    out_re = right_product(first_re, table_re) - right_product(first_im, table_im)
    out_im = right_product(first_re, table_im) + right_product(first_im, table_re)
    return (out_re, out_im)


def dft_tables(length):
    indices = jnp.arange(length, dtype=jnp.int32)
    product = indices[:, None] * indices[None, :] % length
    angles = product.astype(jnp.float32) * (2.0 * math.pi / length)
    cosine_table = jnp.cos(angles)
    sine_table = jnp.sin(angles)
    shifted = jnp.where(indices < length // 2, indices, indices - length).astype(jnp.float32)
    kernel = math.pi * fresnel * shifted * shifted / length

    def spread(weights):
        first_part = jnp.dot(cosine_table * weights[None, :], cosine_table, precision=highest)
        second_part = jnp.dot(sine_table * weights[None, :], sine_table, precision=highest)
        return (first_part + second_part) / length

    near_table = (spread(jnp.cos(kernel)), spread(jnp.sin(kernel)))
    norm_scale = 1.0 / math.sqrt(length)
    far_table = (cosine_table * norm_scale, -sine_table * norm_scale)
    return (near_table, far_table)


def block_tables(table_re, table_im):
    left = jnp.stack([jnp.stack([table_re, -table_im]), jnp.stack([table_im, table_re])])
    right = jnp.stack([jnp.stack([table_re, table_im]), jnp.stack([-table_im, table_re])])
    return (left, right)


def stacked_sandwich(pair, wave_re, wave_im):
    left, right = pair
    wave = jnp.stack([wave_re, wave_im])
    first = jnp.einsum("abmk,bkn->amn", left, wave, precision=highest, preferred_element_type=jnp.float32)
    out = jnp.einsum("bmk,bakn->amn", first, right, precision=highest, preferred_element_type=jnp.float32)
    return (out[0], out[1])


def place(block, offset, total, axis):
    reach = total - block.shape[axis]
    widths = [(0, 0)] * block.ndim
    widths[axis] = (reach, reach)
    return lax.dynamic_slice_in_dim(jnp.pad(block, widths), reach - offset, total, axis=axis)


def likelihood_seed(far_re, far_im, observed):
    intensity = far_re * far_re + far_im * far_im
    shifted_total = intensity + background
    denominator = 1.0 + dead_time * shifted_total
    model_rate = shifted_total / denominator
    slope_term = loss_weight * (1.0 - observed / model_rate) / (denominator * denominator)
    return (2.0 * slope_term * far_re, 2.0 * slope_term * far_im)


def shards(phase_shift, absorption, probe_wave, positions, counts):
    slices_here = phase_shift.shape[0]
    tile_width = phase_shift.shape[2]
    frame_width = probe_wave.shape[1]
    sections = lax.axis_size("section")
    tile_count = lax.axis_size("tile")
    grid_side = math.isqrt(tile_count)
    margin = HALO
    extent = tile_width + 2 * margin
    section_index = lax.axis_index("section")
    column = lax.axis_index("tile") % grid_side
    has_left = (column > 0).astype(jnp.float32)
    has_right = (column < grid_side - 1).astype(jnp.float32)
    own_block = jnp.stack([phase_shift[:, 0], absorption[:, 0]])

    low, high = tile_width - margin, margin
    slices_total = sections * slices_here
    corner = positions[0, 0, 0]
    corner_above = from_behind(corner, "tile", grid_side)
    corner_below = from_behind(corner, "tile", -grid_side)
    to_left = from_behind(own_block[:, :, :, low:], "tile", 1) * has_left
    to_right = from_behind(own_block[:, :, :, :high], "tile", -1) * has_right
    wide = jnp.concatenate([to_left, own_block, to_right], axis=3)
    band_down = lax.dynamic_slice_in_dim(wide[:, :, low:], corner_below[1], frame_width, axis=3)
    band_up = lax.dynamic_slice_in_dim(wide[:, :, :high], corner_above[1], frame_width, axis=3)
    above = from_behind(band_down, "tile", grid_side)
    below = from_behind(band_up, "tile", -grid_side)
    column_band = jnp.concatenate(
        [above, lax.dynamic_slice_in_dim(wide, corner[1], frame_width, axis=3), below], axis=2
    )
    window = lax.dynamic_slice_in_dim(column_band, corner[0], frame_width, axis=2)
    damping = jnp.exp(-window[1])
    own_objects = jnp.stack([damping * jnp.cos(window[0]), damping * jnp.sin(window[0])], axis=1)
    all_objects = lax.all_gather(own_objects, "section", axis=0, tiled=True)
    near_table, far_table = dft_tables(frame_width)
    near_pair = block_tables(*near_table)
    far_pair = block_tables(*far_table)
    near_back = block_tables(near_table[0], -near_table[1])
    far_back = block_tables(far_table[0], -far_table[1])
    observed = counts[0, 0, 0].astype(jnp.float32)
    wave_re, wave_im = probe_wave[0], probe_wave[1]
    exits = []
    for slice_no in range(slices_total):
        object_re = all_objects[slice_no, 0]
        object_im = all_objects[slice_no, 1]
        exit_re = object_re * wave_re - object_im * wave_im
        exit_im = object_re * wave_im + object_im * wave_re
        exits.append((exit_re, exit_im))
        pair = near_pair if slice_no < slices_total - 1 else far_pair
        wave_re, wave_im = stacked_sandwich(pair, exit_re, exit_im)
    grad_re, grad_im = likelihood_seed(wave_re, wave_im, observed)
    terms = []
    for slice_no in reversed(range(slices_total)):
        pair = near_back if slice_no < slices_total - 1 else far_back
        back_re, back_im = stacked_sandwich(pair, grad_re, grad_im)
        exit_re, exit_im = exits[slice_no]
        phase_term = back_im * exit_re - back_re * exit_im
        absorb_term = -(back_re * exit_re + back_im * exit_im)
        terms.append(jnp.stack([phase_term, absorb_term]))
        if slice_no > 0:
            object_re = all_objects[slice_no, 0]
            object_im = all_objects[slice_no, 1]
            grad_re = object_re * back_re + object_im * back_im
            grad_im = object_re * back_im - object_im * back_re
    terms = jnp.stack(terms[::-1], axis=1)
    own_terms = lax.dynamic_slice_in_dim(terms, section_index * slices_here, slices_here, axis=1)
    grad_band = place(own_terms, corner[0], extent, axis=2)
    from_below = from_behind(grad_band[:, :, :margin], "tile", -grid_side)
    from_above = from_behind(grad_band[:, :, margin + tile_width :], "tile", grid_side)
    grad_wide = place(grad_band[:, :, margin : margin + tile_width], corner[1], extent, axis=3)
    grad_wide = grad_wide.at[:, :, low:].add(place(from_below, corner_below[1], extent, axis=3))
    grad_wide = grad_wide.at[:, :, :high].add(place(from_above, corner_above[1], extent, axis=3))
    middle = grad_wide[..., margin : margin + tile_width]
    from_right = from_behind(grad_wide[..., :margin], "tile", -1) * has_right
    from_left = from_behind(grad_wide[..., margin + tile_width :], "tile", 1) * has_left
    middle = middle.at[..., low:].add(from_right)
    middle = middle.at[..., :high].add(from_left)
    half = tile_width // 2
    rep_index = lax.axis_index("rep")
    kept = lax.dynamic_slice_in_dim(middle, rep_index * half, half, axis=2)
    sent = lax.dynamic_slice_in_dim(middle, (1 - rep_index) * half, half, axis=2)
    shares = kept + lax.ppermute(sent, "rep", [(0, 1), (1, 0)])
    return (shares[0][:, None], shares[1][:, None])


def solution(mesh):
    in_specs = (
        P("section", "tile", None, None),
        P("section", "tile", None, None),
        P(),
        P("tile", "rep", None, None),
        P("tile", "rep", None, None, None),
    )
    out_specs = (P("section", "tile", "rep", None), P("section", "tile", "rep", None))
    return jax.shard_map(shards, mesh=mesh, in_specs=in_specs, out_specs=out_specs, check_vma=False)
```

```python
import math

import jax
import jax.numpy as jnp
from jax import lax
from jax.sharding import PartitionSpec as P

HALO = 128


dead_time = 0.1
background = 0.1
loss_weight = 0.1
fresnel = 0.5
highest = lax.Precision.HIGHEST


def from_behind(value, axis, by):
    peers = lax.axis_size(axis)
    pairs = [(i, i + by) for i in range(peers) if 0 <= i + by < peers]
    return lax.ppermute(value, axis, pairs)


def left_product(matrix, frames):
    return jnp.einsum(
        "mk,bkn->bmn", matrix, frames, precision=highest, preferred_element_type=jnp.float32
    )


def right_product(frames, matrix):
    return jnp.einsum(
        "bmk,kn->bmn", frames, matrix, precision=highest, preferred_element_type=jnp.float32
    )


def sandwich(table_re, table_im, wave_re, wave_im):
    first_re = left_product(table_re, wave_re) - left_product(table_im, wave_im)
    first_im = left_product(table_re, wave_im) + left_product(table_im, wave_re)
    out_re = right_product(first_re, table_re) - right_product(first_im, table_im)
    out_im = right_product(first_re, table_im) + right_product(first_im, table_re)
    return (out_re, out_im)


def dft_tables(length):
    indices = jnp.arange(length, dtype=jnp.int32)
    product = indices[:, None] * indices[None, :] % length
    angles = product.astype(jnp.float32) * (2.0 * math.pi / length)
    cosine_table = jnp.cos(angles)
    sine_table = jnp.sin(angles)
    shifted = jnp.where(indices < length // 2, indices, indices - length).astype(jnp.float32)
    kernel = math.pi * fresnel * shifted * shifted / length

    def spread(weights):
        first_part = jnp.dot(cosine_table * weights[None, :], cosine_table, precision=highest)
        second_part = jnp.dot(sine_table * weights[None, :], sine_table, precision=highest)
        return (first_part + second_part) / length

    near_table = (spread(jnp.cos(kernel)), spread(jnp.sin(kernel)))
    norm_scale = 1.0 / math.sqrt(length)
    far_table = (cosine_table * norm_scale, -sine_table * norm_scale)
    return (near_table, far_table)


def block_tables(table_re, table_im):
    left = jnp.stack([jnp.stack([table_re, -table_im]), jnp.stack([table_im, table_re])])
    right = jnp.stack([jnp.stack([table_re, table_im]), jnp.stack([-table_im, table_re])])
    return (left, right)


def stacked_sandwich(pair, wave_re, wave_im):
    left, right = pair
    wave = jnp.stack([wave_re, wave_im])
    first = jnp.einsum("abmk,bkn->amn", left, wave, precision=highest, preferred_element_type=jnp.float32)
    out = jnp.einsum("bmk,bakn->amn", first, right, precision=highest, preferred_element_type=jnp.float32)
    return (out[0], out[1])


def gather_slices(own, sections):
    got = [own]
    for shift in range(1, sections):
        got.append(lax.ppermute(own, "section", [((y + shift) % sections, y) for y in range(sections)]))
    relative = jnp.concatenate(got, axis=0)
    return jnp.roll(relative, lax.axis_index("section") * own.shape[0], axis=0)


def place(block, offset, total, axis):
    reach = total - block.shape[axis]
    widths = [(0, 0)] * block.ndim
    widths[axis] = (reach, reach)
    return lax.dynamic_slice_in_dim(jnp.pad(block, widths), reach - offset, total, axis=axis)


def likelihood_seed(far_re, far_im, observed):
    intensity = far_re * far_re + far_im * far_im
    shifted_total = intensity + background
    denominator = 1.0 + dead_time * shifted_total
    model_rate = shifted_total / denominator
    slope_term = loss_weight * (1.0 - observed / model_rate) / (denominator * denominator)
    return (2.0 * slope_term * far_re, 2.0 * slope_term * far_im)


def shards(phase_shift, absorption, probe_wave, positions, counts):
    slices_here = phase_shift.shape[0]
    tile_width = phase_shift.shape[2]
    frame_width = probe_wave.shape[1]
    sections = lax.axis_size("section")
    tile_count = lax.axis_size("tile")
    grid_side = math.isqrt(tile_count)
    margin = HALO
    extent = tile_width + 2 * margin
    section_index = lax.axis_index("section")
    column = lax.axis_index("tile") % grid_side
    has_left = (column > 0).astype(jnp.float32)
    has_right = (column < grid_side - 1).astype(jnp.float32)
    own_block = jnp.stack([phase_shift[:, 0], absorption[:, 0]])

    low, high = tile_width - margin, margin
    slices_total = sections * slices_here
    corner = positions[0, 0, 0]
    corner_above = from_behind(corner, "tile", grid_side)
    corner_below = from_behind(corner, "tile", -grid_side)
    to_left = from_behind(own_block[:, :, :, low:], "tile", 1) * has_left
    to_right = from_behind(own_block[:, :, :, :high], "tile", -1) * has_right
    wide = jnp.concatenate([to_left, own_block, to_right], axis=3)
    band_down = lax.dynamic_slice_in_dim(wide[:, :, low:], corner_below[1], frame_width, axis=3)
    band_up = lax.dynamic_slice_in_dim(wide[:, :, :high], corner_above[1], frame_width, axis=3)
    above = from_behind(band_down, "tile", grid_side)
    below = from_behind(band_up, "tile", -grid_side)
    column_band = jnp.concatenate(
        [above, lax.dynamic_slice_in_dim(wide, corner[1], frame_width, axis=3), below], axis=2
    )
    window = lax.dynamic_slice_in_dim(column_band, corner[0], frame_width, axis=2)
    damping = jnp.exp(-window[1])
    own_objects = jnp.stack([damping * jnp.cos(window[0]), damping * jnp.sin(window[0])], axis=1)
    all_objects = gather_slices(own_objects, sections)
    near_table, far_table = dft_tables(frame_width)
    near_pair = block_tables(*near_table)
    far_pair = block_tables(*far_table)
    near_back = block_tables(near_table[0], -near_table[1])
    far_back = block_tables(far_table[0], -far_table[1])
    observed = counts[0, 0, 0].astype(jnp.float32)
    wave_re, wave_im = probe_wave[0], probe_wave[1]
    exits = []
    for slice_no in range(slices_total):
        object_re = all_objects[slice_no, 0]
        object_im = all_objects[slice_no, 1]
        exit_re = object_re * wave_re - object_im * wave_im
        exit_im = object_re * wave_im + object_im * wave_re
        exits.append((exit_re, exit_im))
        pair = near_pair if slice_no < slices_total - 1 else far_pair
        wave_re, wave_im = stacked_sandwich(pair, exit_re, exit_im)
    grad_re, grad_im = likelihood_seed(wave_re, wave_im, observed)
    terms = []
    for slice_no in reversed(range(slices_total)):
        pair = near_back if slice_no < slices_total - 1 else far_back
        back_re, back_im = stacked_sandwich(pair, grad_re, grad_im)
        exit_re, exit_im = exits[slice_no]
        phase_term = back_im * exit_re - back_re * exit_im
        absorb_term = -(back_re * exit_re + back_im * exit_im)
        terms.append(jnp.stack([phase_term, absorb_term]))
        if slice_no > 0:
            object_re = all_objects[slice_no, 0]
            object_im = all_objects[slice_no, 1]
            grad_re = object_re * back_re + object_im * back_im
            grad_im = object_re * back_im - object_im * back_re
    terms = jnp.stack(terms[::-1], axis=1)
    own_terms = lax.dynamic_slice_in_dim(terms, section_index * slices_here, slices_here, axis=1)
    grad_band = place(own_terms, corner[0], extent, axis=2)
    from_below = from_behind(grad_band[:, :, :margin], "tile", -grid_side)
    from_above = from_behind(grad_band[:, :, margin + tile_width :], "tile", grid_side)
    grad_wide = place(grad_band[:, :, margin : margin + tile_width], corner[1], extent, axis=3)
    grad_wide = grad_wide.at[:, :, low:].add(place(from_below, corner_below[1], extent, axis=3))
    grad_wide = grad_wide.at[:, :, :high].add(place(from_above, corner_above[1], extent, axis=3))
    middle = grad_wide[..., margin : margin + tile_width]
    from_right = from_behind(grad_wide[..., :margin], "tile", -1) * has_right
    from_left = from_behind(grad_wide[..., margin + tile_width :], "tile", 1) * has_left
    middle = middle.at[..., low:].add(from_right)
    middle = middle.at[..., :high].add(from_left)
    half = tile_width // 2
    rep_index = lax.axis_index("rep")
    kept = lax.dynamic_slice_in_dim(middle, rep_index * half, half, axis=2)
    sent = lax.dynamic_slice_in_dim(middle, (1 - rep_index) * half, half, axis=2)
    shares = kept + lax.ppermute(sent, "rep", [(0, 1), (1, 0)])
    return (shares[0][:, None], shares[1][:, None])


def solution(mesh):
    in_specs = (
        P("section", "tile", None, None),
        P("section", "tile", None, None),
        P(),
        P("tile", "rep", None, None),
        P("tile", "rep", None, None, None),
    )
    out_specs = (P("section", "tile", "rep", None), P("section", "tile", "rep", None))
    return jax.shard_map(shards, mesh=mesh, in_specs=in_specs, out_specs=out_specs, check_vma=False)
```

```python
import math

import jax
import jax.numpy as jnp
from jax import lax
from jax.sharding import PartitionSpec as P

HALO = 128


dead_time = 0.1
background = 0.1
loss_weight = 0.1
fresnel = 0.5
highest = lax.Precision.HIGHEST


def from_behind(value, axis, by):
    peers = lax.axis_size(axis)
    pairs = [(i, i + by) for i in range(peers) if 0 <= i + by < peers]
    return lax.ppermute(value, axis, pairs)


def left_product(matrix, frames):
    return jnp.einsum(
        "mk,bkn->bmn", matrix, frames, precision=highest, preferred_element_type=jnp.float32
    )


def right_product(frames, matrix):
    return jnp.einsum(
        "bmk,kn->bmn", frames, matrix, precision=highest, preferred_element_type=jnp.float32
    )


def sandwich(table_re, table_im, wave_re, wave_im):
    first_re = left_product(table_re, wave_re) - left_product(table_im, wave_im)
    first_im = left_product(table_re, wave_im) + left_product(table_im, wave_re)
    out_re = right_product(first_re, table_re) - right_product(first_im, table_im)
    out_im = right_product(first_re, table_im) + right_product(first_im, table_re)
    return (out_re, out_im)


def dft_tables(length):
    indices = jnp.arange(length, dtype=jnp.int32)
    product = indices[:, None] * indices[None, :] % length
    angles = product.astype(jnp.float32) * (2.0 * math.pi / length)
    cosine_table = jnp.cos(angles)
    sine_table = jnp.sin(angles)
    shifted = jnp.where(indices < length // 2, indices, indices - length).astype(jnp.float32)
    kernel = math.pi * fresnel * shifted * shifted / length

    def spread(weights):
        first_part = jnp.dot(cosine_table * weights[None, :], cosine_table, precision=highest)
        second_part = jnp.dot(sine_table * weights[None, :], sine_table, precision=highest)
        return (first_part + second_part) / length

    near_table = (spread(jnp.cos(kernel)), spread(jnp.sin(kernel)))
    norm_scale = 1.0 / math.sqrt(length)
    far_table = (cosine_table * norm_scale, -sine_table * norm_scale)
    return (near_table, far_table)


def block_tables(table_re, table_im):
    left = jnp.stack([jnp.stack([table_re, -table_im]), jnp.stack([table_im, table_re])])
    right = jnp.stack([jnp.stack([table_re, table_im]), jnp.stack([-table_im, table_re])])
    return (left, right)


def stacked_sandwich(pair, wave_re, wave_im):
    left, right = pair
    wave = jnp.stack([wave_re, wave_im])
    first = jnp.einsum("abmk,bkn->amn", left, wave, precision=highest, preferred_element_type=jnp.float32)
    out = jnp.einsum("bmk,bakn->amn", first, right, precision=highest, preferred_element_type=jnp.float32)
    return (out[0], out[1])


def place(block, offset, total, axis):
    reach = total - block.shape[axis]
    widths = [(0, 0)] * block.ndim
    widths[axis] = (reach, reach)
    return lax.dynamic_slice_in_dim(jnp.pad(block, widths), reach - offset, total, axis=axis)


def likelihood_seed(far_re, far_im, observed):
    intensity = far_re * far_re + far_im * far_im
    shifted_total = intensity + background
    denominator = 1.0 + dead_time * shifted_total
    model_rate = shifted_total / denominator
    slope_term = loss_weight * (1.0 - observed / model_rate) / (denominator * denominator)
    return (2.0 * slope_term * far_re, 2.0 * slope_term * far_im)


def shards(phase_shift, absorption, probe_wave, positions, counts):
    slices_here = phase_shift.shape[0]
    tile_width = phase_shift.shape[2]
    frame_width = probe_wave.shape[1]
    sections = lax.axis_size("section")
    tile_count = lax.axis_size("tile")
    grid_side = math.isqrt(tile_count)
    margin = HALO
    extent = tile_width + 2 * margin
    section_index = lax.axis_index("section")
    column = lax.axis_index("tile") % grid_side
    has_left = (column > 0).astype(jnp.float32)
    has_right = (column < grid_side - 1).astype(jnp.float32)
    own_block = jnp.stack([phase_shift[:, 0], absorption[:, 0]])

    low, high = tile_width - margin, margin
    slices_total = sections * slices_here
    corner = positions[0, 0, 0]
    corner_above = from_behind(corner, "tile", grid_side)
    corner_below = from_behind(corner, "tile", -grid_side)
    to_left = from_behind(own_block[:, :, :, low:], "tile", 1) * has_left
    to_right = from_behind(own_block[:, :, :, :high], "tile", -1) * has_right
    wide = jnp.concatenate([to_left, own_block, to_right], axis=3)
    band_down = lax.dynamic_slice_in_dim(wide[:, :, low:], corner_below[1], frame_width, axis=3)
    band_up = lax.dynamic_slice_in_dim(wide[:, :, :high], corner_above[1], frame_width, axis=3)
    above = from_behind(band_down, "tile", grid_side)
    below = from_behind(band_up, "tile", -grid_side)
    column_band = jnp.concatenate(
        [above, lax.dynamic_slice_in_dim(wide, corner[1], frame_width, axis=3), below], axis=2
    )
    window = lax.dynamic_slice_in_dim(column_band, corner[0], frame_width, axis=2)
    damping = jnp.exp(-window[1])
    own_objects = jnp.stack([damping * jnp.cos(window[0]), damping * jnp.sin(window[0])], axis=1)
    near_table, far_table = lax.optimization_barrier(dft_tables(frame_width))
    near_pair = block_tables(*near_table)
    far_pair = block_tables(*far_table)
    near_back = block_tables(near_table[0], -near_table[1])
    far_back = block_tables(far_table[0], -far_table[1])
    observed = counts[0, 0, 0].astype(jnp.float32)
    wave_re, wave_im = probe_wave[0], probe_wave[1]
    exits = [None] * slices_here
    for stage in range(sections):
        if stage > 0:
            wave_re, wave_im = lax.ppermute(jnp.stack([wave_re, wave_im]), "section", [(stage - 1, stage)])
        is_mine = section_index == stage
        for local in range(slices_here):
            object_re = own_objects[local, 0]
            object_im = own_objects[local, 1]
            exit_re = object_re * wave_re - object_im * wave_im
            exit_im = object_re * wave_im + object_im * wave_re
            if stage == 0:
                exits[local] = (exit_re, exit_im)
            else:
                exits[local] = (
                    jnp.where(is_mine, exit_re, exits[local][0]),
                    jnp.where(is_mine, exit_im, exits[local][1]),
                )
            last = stage == sections - 1 and local == slices_here - 1
            wave_re, wave_im = stacked_sandwich(far_pair if last else near_pair, exit_re, exit_im)
    grad_re, grad_im = likelihood_seed(wave_re, wave_im, observed)
    terms = [None] * slices_here
    for stage in reversed(range(sections)):
        if stage < sections - 1:
            grad_re, grad_im = lax.ppermute(jnp.stack([grad_re, grad_im]), "section", [(stage + 1, stage)])
        is_mine = section_index == stage
        for local in reversed(range(slices_here)):
            last = stage == sections - 1 and local == slices_here - 1
            back_re, back_im = stacked_sandwich(far_back if last else near_back, grad_re, grad_im)
            exit_re, exit_im = exits[local]
            phase_term = back_im * exit_re - back_re * exit_im
            absorb_term = -(back_re * exit_re + back_im * exit_im)
            term = jnp.stack([phase_term, absorb_term])
            terms[local] = term if terms[local] is None else jnp.where(is_mine, term, terms[local])
            if stage > 0 or local > 0:
                object_re = own_objects[local, 0]
                object_im = own_objects[local, 1]
                grad_re = object_re * back_re + object_im * back_im
                grad_im = object_re * back_im - object_im * back_re
    own_terms = jnp.stack(terms, axis=1)
    grad_band = place(own_terms, corner[0], extent, axis=2)
    from_below = from_behind(grad_band[:, :, :margin], "tile", -grid_side)
    from_above = from_behind(grad_band[:, :, margin + tile_width :], "tile", grid_side)
    grad_wide = place(grad_band[:, :, margin : margin + tile_width], corner[1], extent, axis=3)
    grad_wide = grad_wide.at[:, :, low:].add(place(from_below, corner_below[1], extent, axis=3))
    grad_wide = grad_wide.at[:, :, :high].add(place(from_above, corner_above[1], extent, axis=3))
    middle = grad_wide[..., margin : margin + tile_width]
    from_right = from_behind(grad_wide[..., :margin], "tile", -1) * has_right
    from_left = from_behind(grad_wide[..., margin + tile_width :], "tile", 1) * has_left
    middle = middle.at[..., low:].add(from_right)
    middle = middle.at[..., :high].add(from_left)
    half = tile_width // 2
    rep_index = lax.axis_index("rep")
    kept = lax.dynamic_slice_in_dim(middle, rep_index * half, half, axis=2)
    sent = lax.dynamic_slice_in_dim(middle, (1 - rep_index) * half, half, axis=2)
    shares = kept + lax.ppermute(sent, "rep", [(0, 1), (1, 0)])
    return (shares[0][:, None], shares[1][:, None])


def solution(mesh):
    in_specs = (
        P("section", "tile", None, None),
        P("section", "tile", None, None),
        P(),
        P("tile", "rep", None, None),
        P("tile", "rep", None, None, None),
    )
    out_specs = (P("section", "tile", "rep", None), P("section", "tile", "rep", None))
    return jax.shard_map(shards, mesh=mesh, in_specs=in_specs, out_specs=out_specs, check_vma=False)
```

```python
import math

import jax
import jax.numpy as jnp
from jax import lax
from jax.sharding import PartitionSpec as P

HALO = 128


dead_time = 0.1
background = 0.1
loss_weight = 0.1
fresnel = 0.5
highest = lax.Precision.HIGHEST


def from_behind(value, axis, by):
    peers = lax.axis_size(axis)
    pairs = [(i, i + by) for i in range(peers) if 0 <= i + by < peers]
    return lax.ppermute(value, axis, pairs)


def left_product(matrix, frames):
    return jnp.einsum(
        "mk,bkn->bmn", matrix, frames, precision=highest, preferred_element_type=jnp.float32
    )


def right_product(frames, matrix):
    return jnp.einsum(
        "bmk,kn->bmn", frames, matrix, precision=highest, preferred_element_type=jnp.float32
    )


def sandwich(table_re, table_im, wave_re, wave_im):
    first_re = left_product(table_re, wave_re) - left_product(table_im, wave_im)
    first_im = left_product(table_re, wave_im) + left_product(table_im, wave_re)
    out_re = right_product(first_re, table_re) - right_product(first_im, table_im)
    out_im = right_product(first_re, table_im) + right_product(first_im, table_re)
    return (out_re, out_im)


def dft_tables(length):
    indices = jnp.arange(length, dtype=jnp.int32)
    product = indices[:, None] * indices[None, :] % length
    angles = product.astype(jnp.float32) * (2.0 * math.pi / length)
    cosine_table = jnp.cos(angles)
    sine_table = jnp.sin(angles)
    shifted = jnp.where(indices < length // 2, indices, indices - length).astype(jnp.float32)
    kernel = math.pi * fresnel * shifted * shifted / length

    def spread(weights):
        first_part = jnp.dot(cosine_table * weights[None, :], cosine_table, precision=highest)
        second_part = jnp.dot(sine_table * weights[None, :], sine_table, precision=highest)
        return (first_part + second_part) / length

    near_table = (spread(jnp.cos(kernel)), spread(jnp.sin(kernel)))
    norm_scale = 1.0 / math.sqrt(length)
    far_table = (cosine_table * norm_scale, -sine_table * norm_scale)
    return (near_table, far_table)


def block_tables(table_re, table_im):
    left = jnp.stack([jnp.stack([table_re, -table_im]), jnp.stack([table_im, table_re])])
    right = jnp.stack([jnp.stack([table_re, table_im]), jnp.stack([-table_im, table_re])])
    return (left, right)


def stacked_sandwich(pair, wave_re, wave_im):
    left, right = pair
    wave = jnp.stack([wave_re, wave_im])
    first = jnp.einsum("abmk,bkn->amn", left, wave, precision=highest, preferred_element_type=jnp.float32)
    out = jnp.einsum("bmk,bakn->amn", first, right, precision=highest, preferred_element_type=jnp.float32)
    return (out[0], out[1])


def gather_slices(own, sections):
    got = [own]
    for shift in range(1, sections):
        got.append(lax.ppermute(own, "section", [((y + shift) % sections, y) for y in range(sections)]))
    here = lax.axis_index("section")
    ordered = []
    for wanted in range(sections):
        pick = got[0]
        for shift in range(1, sections):
            pick = jnp.where((here + shift) % sections == wanted, got[shift], pick)
        ordered.append(pick)
    return jnp.concatenate(ordered, axis=0)


def place(block, offset, total, axis):
    reach = total - block.shape[axis]
    widths = [(0, 0)] * block.ndim
    widths[axis] = (reach, reach)
    return lax.dynamic_slice_in_dim(jnp.pad(block, widths), reach - offset, total, axis=axis)


def likelihood_seed(far_re, far_im, observed):
    intensity = far_re * far_re + far_im * far_im
    shifted_total = intensity + background
    denominator = 1.0 + dead_time * shifted_total
    model_rate = shifted_total / denominator
    slope_term = loss_weight * (1.0 - observed / model_rate) / (denominator * denominator)
    return (2.0 * slope_term * far_re, 2.0 * slope_term * far_im)


def shards(phase_shift, absorption, probe_wave, positions, counts):
    slices_here = phase_shift.shape[0]
    tile_width = phase_shift.shape[2]
    frame_width = probe_wave.shape[1]
    sections = lax.axis_size("section")
    tile_count = lax.axis_size("tile")
    grid_side = math.isqrt(tile_count)
    margin = HALO
    extent = tile_width + 2 * margin
    section_index = lax.axis_index("section")
    column = lax.axis_index("tile") % grid_side
    has_left = (column > 0).astype(jnp.float32)
    has_right = (column < grid_side - 1).astype(jnp.float32)
    own_block = jnp.stack([phase_shift[:, 0], absorption[:, 0]])

    low, high = tile_width - margin, margin
    slices_total = sections * slices_here
    corner = positions[0, 0, 0]
    corner_above = from_behind(corner, "tile", grid_side)
    corner_below = from_behind(corner, "tile", -grid_side)
    to_left = from_behind(own_block[:, :, :, low:], "tile", 1) * has_left
    to_right = from_behind(own_block[:, :, :, :high], "tile", -1) * has_right
    wide = jnp.concatenate([to_left, own_block, to_right], axis=3)
    band_down = lax.dynamic_slice_in_dim(wide[:, :, low:], corner_below[1], frame_width, axis=3)
    band_up = lax.dynamic_slice_in_dim(wide[:, :, :high], corner_above[1], frame_width, axis=3)
    above = from_behind(band_down, "tile", grid_side)
    below = from_behind(band_up, "tile", -grid_side)
    column_band = jnp.concatenate(
        [above, lax.dynamic_slice_in_dim(wide, corner[1], frame_width, axis=3), below], axis=2
    )
    window = lax.dynamic_slice_in_dim(column_band, corner[0], frame_width, axis=2)
    damping = jnp.exp(-window[1])
    own_objects = jnp.stack([damping * jnp.cos(window[0]), damping * jnp.sin(window[0])], axis=1)
    all_objects = gather_slices(own_objects, sections)
    near_table, far_table = lax.optimization_barrier(dft_tables(frame_width))
    near_pair = block_tables(*near_table)
    far_pair = block_tables(*far_table)
    near_back = block_tables(near_table[0], -near_table[1])
    far_back = block_tables(far_table[0], -far_table[1])
    observed = counts[0, 0, 0].astype(jnp.float32)
    wave_re, wave_im = probe_wave[0], probe_wave[1]
    exits = []
    for slice_no in range(slices_total):
        object_re = all_objects[slice_no, 0]
        object_im = all_objects[slice_no, 1]
        exit_re = object_re * wave_re - object_im * wave_im
        exit_im = object_re * wave_im + object_im * wave_re
        exits.append((exit_re, exit_im))
        pair = near_pair if slice_no < slices_total - 1 else far_pair
        wave_re, wave_im = stacked_sandwich(pair, exit_re, exit_im)
    grad_re, grad_im = likelihood_seed(wave_re, wave_im, observed)
    terms = []
    for slice_no in reversed(range(slices_total)):
        pair = near_back if slice_no < slices_total - 1 else far_back
        back_re, back_im = stacked_sandwich(pair, grad_re, grad_im)
        exit_re, exit_im = exits[slice_no]
        phase_term = back_im * exit_re - back_re * exit_im
        absorb_term = -(back_re * exit_re + back_im * exit_im)
        terms.append(jnp.stack([phase_term, absorb_term]))
        if slice_no > 0:
            object_re = all_objects[slice_no, 0]
            object_im = all_objects[slice_no, 1]
            grad_re = object_re * back_re + object_im * back_im
            grad_im = object_re * back_im - object_im * back_re
    terms = jnp.stack(terms[::-1], axis=1)
    own_terms = lax.dynamic_slice_in_dim(terms, section_index * slices_here, slices_here, axis=1)
    grad_band = place(own_terms, corner[0], extent, axis=2)
    from_below = from_behind(grad_band[:, :, :margin], "tile", -grid_side)
    from_above = from_behind(grad_band[:, :, margin + tile_width :], "tile", grid_side)
    grad_wide = place(grad_band[:, :, margin : margin + tile_width], corner[1], extent, axis=3)
    grad_wide = grad_wide.at[:, :, low:].add(place(from_below, corner_below[1], extent, axis=3))
    grad_wide = grad_wide.at[:, :, :high].add(place(from_above, corner_above[1], extent, axis=3))
    middle = grad_wide[..., margin : margin + tile_width]
    from_right = from_behind(grad_wide[..., :margin], "tile", -1) * has_right
    from_left = from_behind(grad_wide[..., margin + tile_width :], "tile", 1) * has_left
    middle = middle.at[..., low:].add(from_right)
    middle = middle.at[..., :high].add(from_left)
    half = tile_width // 2
    rep_index = lax.axis_index("rep")
    kept = lax.dynamic_slice_in_dim(middle, rep_index * half, half, axis=2)
    sent = lax.dynamic_slice_in_dim(middle, (1 - rep_index) * half, half, axis=2)
    shares = kept + lax.ppermute(sent, "rep", [(0, 1), (1, 0)])
    return (shares[0][:, None], shares[1][:, None])


def solution(mesh):
    in_specs = (
        P("section", "tile", None, None),
        P("section", "tile", None, None),
        P(),
        P("tile", "rep", None, None),
        P("tile", "rep", None, None, None),
    )
    out_specs = (P("section", "tile", "rep", None), P("section", "tile", "rep", None))
    return jax.shard_map(shards, mesh=mesh, in_specs=in_specs, out_specs=out_specs, check_vma=False)
```

```python
import functools
import math

import jax
import jax.numpy as jnp
from jax import lax
from jax.experimental import pallas as pl
from jax.experimental.pallas import tpu as pltpu
from jax.sharding import PartitionSpec as P

MESH = pl.DeviceIdType.MESH

HALO = 128


dead_time = 0.1
background = 0.1
loss_weight = 0.1
fresnel = 0.5
highest = lax.Precision.HIGHEST


def from_behind(value, axis, by):
    peers = lax.axis_size(axis)
    pairs = [(i, i + by) for i in range(peers) if 0 <= i + by < peers]
    return lax.ppermute(value, axis, pairs)


def left_product(matrix, frames):
    return jnp.einsum(
        "mk,bkn->bmn", matrix, frames, precision=highest, preferred_element_type=jnp.float32
    )


def right_product(frames, matrix):
    return jnp.einsum(
        "bmk,kn->bmn", frames, matrix, precision=highest, preferred_element_type=jnp.float32
    )


def sandwich(table_re, table_im, wave_re, wave_im):
    first_re = left_product(table_re, wave_re) - left_product(table_im, wave_im)
    first_im = left_product(table_re, wave_im) + left_product(table_im, wave_re)
    out_re = right_product(first_re, table_re) - right_product(first_im, table_im)
    out_im = right_product(first_re, table_im) + right_product(first_im, table_re)
    return (out_re, out_im)


def dft_tables(length):
    indices = jnp.arange(length, dtype=jnp.int32)
    product = indices[:, None] * indices[None, :] % length
    angles = product.astype(jnp.float32) * (2.0 * math.pi / length)
    cosine_table = jnp.cos(angles)
    sine_table = jnp.sin(angles)
    shifted = jnp.where(indices < length // 2, indices, indices - length).astype(jnp.float32)
    kernel = math.pi * fresnel * shifted * shifted / length

    def spread(weights):
        first_part = jnp.dot(cosine_table * weights[None, :], cosine_table, precision=highest)
        second_part = jnp.dot(sine_table * weights[None, :], sine_table, precision=highest)
        return (first_part + second_part) / length

    near_table = (spread(jnp.cos(kernel)), spread(jnp.sin(kernel)))
    norm_scale = 1.0 / math.sqrt(length)
    far_table = (cosine_table * norm_scale, -sine_table * norm_scale)
    return (near_table, far_table)


def block_tables(table_re, table_im):
    left = jnp.stack([jnp.stack([table_re, -table_im]), jnp.stack([table_im, table_re])])
    right = jnp.stack([jnp.stack([table_re, table_im]), jnp.stack([-table_im, table_re])])
    return (left, right)


def stacked_sandwich(pair, wave_re, wave_im):
    left, right = pair
    wave = jnp.stack([wave_re, wave_im])
    first = jnp.einsum("abmk,bkn->amn", left, wave, precision=highest, preferred_element_type=jnp.float32)
    out = jnp.einsum("bmk,bakn->amn", first, right, precision=highest, preferred_element_type=jnp.float32)
    return (out[0], out[1])


def exchange_kernel(peers, own_ref, out_ref, held, send_sem, recv_sem):
    me = lax.axis_index("section")
    tile = lax.axis_index("tile")
    rep = lax.axis_index("rep")
    barrier = pltpu.get_barrier_semaphore()
    for shift in range(1, peers):
        pl.semaphore_signal(
            barrier, inc=1, device_id=(lax.rem(me + shift, peers), tile, rep), device_id_type=MESH
        )
    pl.semaphore_wait(barrier, peers - 1)
    copies = []
    for shift in range(1, peers):
        copy = pltpu.make_async_remote_copy(
            src_ref=own_ref,
            dst_ref=held.at[shift - 1],
            send_sem=send_sem.at[shift - 1],
            recv_sem=recv_sem.at[shift - 1],
            device_id=(lax.rem(me + peers - shift, peers), tile, rep),
            device_id_type=MESH,
        )
        copy.start()
        copies.append(copy)
    for copy in copies:
        copy.wait()
    out_ref[...] = held[...]


def gather_slices(own, sections):
    received = pl.pallas_call(
        functools.partial(exchange_kernel, sections),
        out_shape=jax.ShapeDtypeStruct((sections - 1,) + own.shape, own.dtype),
        in_specs=[pl.BlockSpec(memory_space=pltpu.VMEM)],
        out_specs=pl.BlockSpec(memory_space=pltpu.VMEM),
        scratch_shapes=[
            pltpu.VMEM((sections - 1,) + own.shape, own.dtype),
            pltpu.SemaphoreType.DMA((sections - 1,)),
            pltpu.SemaphoreType.DMA((sections - 1,)),
        ],
        compiler_params=pltpu.CompilerParams(collective_id=0, has_side_effects=True),
    )(own)
    got = [own] + [received[shift - 1] for shift in range(1, sections)]
    here = lax.axis_index("section")
    ordered = []
    for wanted in range(sections):
        pick = got[0]
        for shift in range(1, sections):
            pick = jnp.where((here + shift) % sections == wanted, got[shift], pick)
        ordered.append(pick)
    return jnp.concatenate(ordered, axis=0)


def place(block, offset, total, axis):
    reach = total - block.shape[axis]
    widths = [(0, 0)] * block.ndim
    widths[axis] = (reach, reach)
    return lax.dynamic_slice_in_dim(jnp.pad(block, widths), reach - offset, total, axis=axis)


def likelihood_seed(far_re, far_im, observed):
    intensity = far_re * far_re + far_im * far_im
    shifted_total = intensity + background
    denominator = 1.0 + dead_time * shifted_total
    model_rate = shifted_total / denominator
    slope_term = loss_weight * (1.0 - observed / model_rate) / (denominator * denominator)
    return (2.0 * slope_term * far_re, 2.0 * slope_term * far_im)


def shards(phase_shift, absorption, probe_wave, positions, counts):
    slices_here = phase_shift.shape[0]
    tile_width = phase_shift.shape[2]
    frame_width = probe_wave.shape[1]
    sections = lax.axis_size("section")
    tile_count = lax.axis_size("tile")
    grid_side = math.isqrt(tile_count)
    margin = HALO
    extent = tile_width + 2 * margin
    section_index = lax.axis_index("section")
    column = lax.axis_index("tile") % grid_side
    has_left = (column > 0).astype(jnp.float32)
    has_right = (column < grid_side - 1).astype(jnp.float32)
    own_block = jnp.stack([phase_shift[:, 0], absorption[:, 0]])

    low, high = tile_width - margin, margin
    slices_total = sections * slices_here
    corner = positions[0, 0, 0]
    corner_above = from_behind(corner, "tile", grid_side)
    corner_below = from_behind(corner, "tile", -grid_side)
    to_left = from_behind(own_block[:, :, :, low:], "tile", 1) * has_left
    to_right = from_behind(own_block[:, :, :, :high], "tile", -1) * has_right
    wide = jnp.concatenate([to_left, own_block, to_right], axis=3)
    band_down = lax.dynamic_slice_in_dim(wide[:, :, low:], corner_below[1], frame_width, axis=3)
    band_up = lax.dynamic_slice_in_dim(wide[:, :, :high], corner_above[1], frame_width, axis=3)
    above = from_behind(band_down, "tile", grid_side)
    below = from_behind(band_up, "tile", -grid_side)
    column_band = jnp.concatenate(
        [above, lax.dynamic_slice_in_dim(wide, corner[1], frame_width, axis=3), below], axis=2
    )
    window = lax.dynamic_slice_in_dim(column_band, corner[0], frame_width, axis=2)
    damping = jnp.exp(-window[1])
    own_objects = jnp.stack([damping * jnp.cos(window[0]), damping * jnp.sin(window[0])], axis=1)
    all_objects = gather_slices(own_objects, sections)
    near_table, far_table = lax.optimization_barrier(dft_tables(frame_width))
    near_pair = block_tables(*near_table)
    far_pair = block_tables(*far_table)
    near_back = block_tables(near_table[0], -near_table[1])
    far_back = block_tables(far_table[0], -far_table[1])
    observed = counts[0, 0, 0].astype(jnp.float32)
    wave_re, wave_im = probe_wave[0], probe_wave[1]
    exits = []
    for slice_no in range(slices_total):
        object_re = all_objects[slice_no, 0]
        object_im = all_objects[slice_no, 1]
        exit_re = object_re * wave_re - object_im * wave_im
        exit_im = object_re * wave_im + object_im * wave_re
        exits.append((exit_re, exit_im))
        pair = near_pair if slice_no < slices_total - 1 else far_pair
        wave_re, wave_im = stacked_sandwich(pair, exit_re, exit_im)
    grad_re, grad_im = likelihood_seed(wave_re, wave_im, observed)
    terms = []
    for slice_no in reversed(range(slices_total)):
        pair = near_back if slice_no < slices_total - 1 else far_back
        back_re, back_im = stacked_sandwich(pair, grad_re, grad_im)
        exit_re, exit_im = exits[slice_no]
        phase_term = back_im * exit_re - back_re * exit_im
        absorb_term = -(back_re * exit_re + back_im * exit_im)
        terms.append(jnp.stack([phase_term, absorb_term]))
        if slice_no > 0:
            object_re = all_objects[slice_no, 0]
            object_im = all_objects[slice_no, 1]
            grad_re = object_re * back_re + object_im * back_im
            grad_im = object_re * back_im - object_im * back_re
    terms = jnp.stack(terms[::-1], axis=1)
    own_terms = lax.dynamic_slice_in_dim(terms, section_index * slices_here, slices_here, axis=1)
    grad_band = place(own_terms, corner[0], extent, axis=2)
    from_below = from_behind(grad_band[:, :, :margin], "tile", -grid_side)
    from_above = from_behind(grad_band[:, :, margin + tile_width :], "tile", grid_side)
    grad_wide = place(grad_band[:, :, margin : margin + tile_width], corner[1], extent, axis=3)
    grad_wide = grad_wide.at[:, :, low:].add(place(from_below, corner_below[1], extent, axis=3))
    grad_wide = grad_wide.at[:, :, :high].add(place(from_above, corner_above[1], extent, axis=3))
    middle = grad_wide[..., margin : margin + tile_width]
    from_right = from_behind(grad_wide[..., :margin], "tile", -1) * has_right
    from_left = from_behind(grad_wide[..., margin + tile_width :], "tile", 1) * has_left
    middle = middle.at[..., low:].add(from_right)
    middle = middle.at[..., :high].add(from_left)
    half = tile_width // 2
    rep_index = lax.axis_index("rep")
    kept = lax.dynamic_slice_in_dim(middle, rep_index * half, half, axis=2)
    sent = lax.dynamic_slice_in_dim(middle, (1 - rep_index) * half, half, axis=2)
    shares = kept + lax.ppermute(sent, "rep", [(0, 1), (1, 0)])
    return (shares[0][:, None], shares[1][:, None])


def solution(mesh):
    in_specs = (
        P("section", "tile", None, None),
        P("section", "tile", None, None),
        P(),
        P("tile", "rep", None, None),
        P("tile", "rep", None, None, None),
    )
    out_specs = (P("section", "tile", "rep", None), P("section", "tile", "rep", None))
    return jax.shard_map(shards, mesh=mesh, in_specs=in_specs, out_specs=out_specs, check_vma=False)
```

```python
import functools
import math

import jax
import jax.numpy as jnp
from jax import lax
from jax.experimental import pallas as pl
from jax.experimental.pallas import tpu as pltpu
from jax.sharding import PartitionSpec as P

MESH = pl.DeviceIdType.MESH

HALO = 128


dead_time = 0.1
background = 0.1
loss_weight = 0.1
fresnel = 0.5
highest = lax.Precision.HIGHEST


def from_behind(value, axis, by):
    peers = lax.axis_size(axis)
    pairs = [(i, i + by) for i in range(peers) if 0 <= i + by < peers]
    return lax.ppermute(value, axis, pairs)


def left_product(matrix, frames):
    return jnp.einsum(
        "mk,bkn->bmn", matrix, frames, precision=highest, preferred_element_type=jnp.float32
    )


def right_product(frames, matrix):
    return jnp.einsum(
        "bmk,kn->bmn", frames, matrix, precision=highest, preferred_element_type=jnp.float32
    )


def sandwich(table_re, table_im, wave_re, wave_im):
    first_re = left_product(table_re, wave_re) - left_product(table_im, wave_im)
    first_im = left_product(table_re, wave_im) + left_product(table_im, wave_re)
    out_re = right_product(first_re, table_re) - right_product(first_im, table_im)
    out_im = right_product(first_re, table_im) + right_product(first_im, table_re)
    return (out_re, out_im)


def dft_tables(length):
    indices = jnp.arange(length, dtype=jnp.int32)
    product = indices[:, None] * indices[None, :] % length
    angles = product.astype(jnp.float32) * (2.0 * math.pi / length)
    cosine_table = jnp.cos(angles)
    sine_table = jnp.sin(angles)
    shifted = jnp.where(indices < length // 2, indices, indices - length).astype(jnp.float32)
    kernel = math.pi * fresnel * shifted * shifted / length

    def spread(weights):
        first_part = jnp.dot(cosine_table * weights[None, :], cosine_table, precision=highest)
        second_part = jnp.dot(sine_table * weights[None, :], sine_table, precision=highest)
        return (first_part + second_part) / length

    near_table = (spread(jnp.cos(kernel)), spread(jnp.sin(kernel)))
    norm_scale = 1.0 / math.sqrt(length)
    far_table = (cosine_table * norm_scale, -sine_table * norm_scale)
    return (near_table, far_table)


def block_tables(table_re, table_im):
    left = jnp.stack([jnp.stack([table_re, -table_im]), jnp.stack([table_im, table_re])])
    right = jnp.stack([jnp.stack([table_re, table_im]), jnp.stack([-table_im, table_re])])
    return (left, right)


def stacked_sandwich(pair, wave_re, wave_im):
    left, right = pair
    wave = jnp.stack([wave_re, wave_im])
    first = jnp.einsum("abmk,bkn->amn", left, wave, precision=highest, preferred_element_type=jnp.float32)
    out = jnp.einsum("bmk,bakn->amn", first, right, precision=highest, preferred_element_type=jnp.float32)
    return (out[0], out[1])


def exchange_kernel(peers, own_ref, out_ref, held, send_sem, recv_sem):
    me = lax.axis_index("section")
    tile = lax.axis_index("tile")
    rep = lax.axis_index("rep")
    barrier = pltpu.get_barrier_semaphore()
    for shift in range(1, peers):
        pl.semaphore_signal(
            barrier, inc=1, device_id=(lax.rem(me + shift, peers), tile, rep), device_id_type=MESH
        )
    pl.semaphore_wait(barrier, peers - 1)
    copies = []
    for shift in range(1, peers):
        copy = pltpu.make_async_remote_copy(
            src_ref=own_ref,
            dst_ref=held.at[shift - 1],
            send_sem=send_sem.at[shift - 1],
            recv_sem=recv_sem.at[shift - 1],
            device_id=(lax.rem(me + peers - shift, peers), tile, rep),
            device_id_type=MESH,
        )
        copy.start()
        copies.append(copy)
    for copy in copies:
        copy.wait()
    out_ref[...] = held[...]


def neighbour_kernel(moves, sizes, *refs):
    count = len(moves)
    sources, outs, held = refs[:count], refs[count : 2 * count], refs[2 * count : 3 * count]
    send_sem, recv_sem = refs[3 * count], refs[3 * count + 1]
    here = {axis: lax.axis_index(axis) for axis in ("section", "tile", "rep")}

    def target(move):
        axis, shift = move
        coords = dict(here)
        coords[axis] = lax.rem(here[axis] + shift + sizes[axis], sizes[axis])
        return (coords["section"], coords["tile"], coords["rep"])

    partners = []
    for move in moves:
        if move not in partners:
            partners.append(move)
    barrier = pltpu.get_barrier_semaphore()
    for move in partners:
        pl.semaphore_signal(barrier, inc=1, device_id=target(move), device_id_type=MESH)
    pl.semaphore_wait(barrier, len(partners))
    copies = []
    for lane, move in enumerate(moves):
        copy = pltpu.make_async_remote_copy(
            src_ref=sources[lane],
            dst_ref=held[lane],
            send_sem=send_sem.at[lane],
            recv_sem=recv_sem.at[lane],
            device_id=target(move),
            device_id_type=MESH,
        )
        copy.start()
        copies.append(copy)
    for copy in copies:
        copy.wait()
    for lane in range(count):
        outs[lane][...] = held[lane][...]


def exchange(blocks, moves, sizes, ident):
    count = len(blocks)
    vmem = pl.BlockSpec(memory_space=pltpu.VMEM)
    return pl.pallas_call(
        functools.partial(neighbour_kernel, tuple(moves), sizes),
        out_shape=[jax.ShapeDtypeStruct(b.shape, b.dtype) for b in blocks],
        in_specs=[vmem] * count,
        out_specs=[vmem] * count,
        scratch_shapes=[pltpu.VMEM(b.shape, b.dtype) for b in blocks]
        + [pltpu.SemaphoreType.DMA((count,)), pltpu.SemaphoreType.DMA((count,))],
        compiler_params=pltpu.CompilerParams(collective_id=ident, has_side_effects=True),
    )(*blocks)


def gather_slices(own, sections):
    received = pl.pallas_call(
        functools.partial(exchange_kernel, sections),
        out_shape=jax.ShapeDtypeStruct((sections - 1,) + own.shape, own.dtype),
        in_specs=[pl.BlockSpec(memory_space=pltpu.VMEM)],
        out_specs=pl.BlockSpec(memory_space=pltpu.VMEM),
        scratch_shapes=[
            pltpu.VMEM((sections - 1,) + own.shape, own.dtype),
            pltpu.SemaphoreType.DMA((sections - 1,)),
            pltpu.SemaphoreType.DMA((sections - 1,)),
        ],
        compiler_params=pltpu.CompilerParams(collective_id=0, has_side_effects=True),
    )(own)
    got = [own] + [received[shift - 1] for shift in range(1, sections)]
    here = lax.axis_index("section")
    ordered = []
    for wanted in range(sections):
        pick = got[0]
        for shift in range(1, sections):
            pick = jnp.where((here + shift) % sections == wanted, got[shift], pick)
        ordered.append(pick)
    return jnp.concatenate(ordered, axis=0)


def place(block, offset, total, axis):
    reach = total - block.shape[axis]
    widths = [(0, 0)] * block.ndim
    widths[axis] = (reach, reach)
    return lax.dynamic_slice_in_dim(jnp.pad(block, widths), reach - offset, total, axis=axis)


def likelihood_seed(far_re, far_im, observed):
    intensity = far_re * far_re + far_im * far_im
    shifted_total = intensity + background
    denominator = 1.0 + dead_time * shifted_total
    model_rate = shifted_total / denominator
    slope_term = loss_weight * (1.0 - observed / model_rate) / (denominator * denominator)
    return (2.0 * slope_term * far_re, 2.0 * slope_term * far_im)


def shards(phase_shift, absorption, probe_wave, positions, counts):
    slices_here = phase_shift.shape[0]
    tile_width = phase_shift.shape[2]
    frame_width = probe_wave.shape[1]
    sections = lax.axis_size("section")
    tile_count = lax.axis_size("tile")
    grid_side = math.isqrt(tile_count)
    margin = HALO
    extent = tile_width + 2 * margin
    section_index = lax.axis_index("section")
    column = lax.axis_index("tile") % grid_side
    has_left = (column > 0).astype(jnp.float32)
    has_right = (column < grid_side - 1).astype(jnp.float32)
    own_block = jnp.stack([phase_shift[:, 0], absorption[:, 0]])

    low, high = tile_width - margin, margin
    slices_total = sections * slices_here
    corner = positions[0, 0, 0]
    corner_above = from_behind(corner, "tile", grid_side)
    corner_below = from_behind(corner, "tile", -grid_side)
    sizes = {"section": sections, "tile": tile_count, "rep": lax.axis_size("rep")}
    row = lax.axis_index("tile") // grid_side
    has_above = (row > 0).astype(jnp.float32)
    has_below = (row < grid_side - 1).astype(jnp.float32)
    to_left, to_right = exchange(
        [own_block[:, :, :, low:], own_block[:, :, :, :high]], [("tile", 1), ("tile", -1)], sizes, 1
    )
    to_left = to_left * has_left
    to_right = to_right * has_right
    wide = jnp.concatenate([to_left, own_block, to_right], axis=3)
    band_down = lax.dynamic_slice_in_dim(wide[:, :, low:], corner_below[1], frame_width, axis=3)
    band_up = lax.dynamic_slice_in_dim(wide[:, :, :high], corner_above[1], frame_width, axis=3)
    above, below = exchange([band_down, band_up], [("tile", grid_side), ("tile", -grid_side)], sizes, 2)
    above = above * has_above
    below = below * has_below
    column_band = jnp.concatenate(
        [above, lax.dynamic_slice_in_dim(wide, corner[1], frame_width, axis=3), below], axis=2
    )
    window = lax.dynamic_slice_in_dim(column_band, corner[0], frame_width, axis=2)
    damping = jnp.exp(-window[1])
    own_objects = jnp.stack([damping * jnp.cos(window[0]), damping * jnp.sin(window[0])], axis=1)
    all_objects = gather_slices(own_objects, sections)
    near_table, far_table = lax.optimization_barrier(dft_tables(frame_width))
    near_pair = block_tables(*near_table)
    far_pair = block_tables(*far_table)
    near_back = block_tables(near_table[0], -near_table[1])
    far_back = block_tables(far_table[0], -far_table[1])
    observed = counts[0, 0, 0].astype(jnp.float32)
    wave_re, wave_im = probe_wave[0], probe_wave[1]
    exits = []
    for slice_no in range(slices_total):
        object_re = all_objects[slice_no, 0]
        object_im = all_objects[slice_no, 1]
        exit_re = object_re * wave_re - object_im * wave_im
        exit_im = object_re * wave_im + object_im * wave_re
        exits.append((exit_re, exit_im))
        pair = near_pair if slice_no < slices_total - 1 else far_pair
        wave_re, wave_im = stacked_sandwich(pair, exit_re, exit_im)
    grad_re, grad_im = likelihood_seed(wave_re, wave_im, observed)
    terms = []
    for slice_no in reversed(range(slices_total)):
        pair = near_back if slice_no < slices_total - 1 else far_back
        back_re, back_im = stacked_sandwich(pair, grad_re, grad_im)
        exit_re, exit_im = exits[slice_no]
        phase_term = back_im * exit_re - back_re * exit_im
        absorb_term = -(back_re * exit_re + back_im * exit_im)
        terms.append(jnp.stack([phase_term, absorb_term]))
        if slice_no > 0:
            object_re = all_objects[slice_no, 0]
            object_im = all_objects[slice_no, 1]
            grad_re = object_re * back_re + object_im * back_im
            grad_im = object_re * back_im - object_im * back_re
    terms = jnp.stack(terms[::-1], axis=1)
    own_terms = lax.dynamic_slice_in_dim(terms, section_index * slices_here, slices_here, axis=1)
    grad_band = place(own_terms, corner[0], extent, axis=2)
    from_below, from_above = exchange(
        [grad_band[:, :, :margin], grad_band[:, :, margin + tile_width :]],
        [("tile", -grid_side), ("tile", grid_side)],
        sizes,
        3,
    )
    from_below = from_below * has_below
    from_above = from_above * has_above
    grad_wide = place(grad_band[:, :, margin : margin + tile_width], corner[1], extent, axis=3)
    grad_wide = grad_wide.at[:, :, low:].add(place(from_below, corner_below[1], extent, axis=3))
    grad_wide = grad_wide.at[:, :, :high].add(place(from_above, corner_above[1], extent, axis=3))
    middle = grad_wide[..., margin : margin + tile_width]
    from_right, from_left = exchange(
        [grad_wide[..., :margin], grad_wide[..., margin + tile_width :]], [("tile", -1), ("tile", 1)], sizes, 4
    )
    from_right = from_right * has_right
    from_left = from_left * has_left
    middle = middle.at[..., low:].add(from_right)
    middle = middle.at[..., :high].add(from_left)
    half = tile_width // 2
    rep_index = lax.axis_index("rep")
    kept = lax.dynamic_slice_in_dim(middle, rep_index * half, half, axis=2)
    sent = lax.dynamic_slice_in_dim(middle, (1 - rep_index) * half, half, axis=2)
    (swapped,) = exchange([sent], [("rep", 1)], sizes, 5)
    shares = kept + swapped
    return (shares[0][:, None], shares[1][:, None])


def solution(mesh):
    in_specs = (
        P("section", "tile", None, None),
        P("section", "tile", None, None),
        P(),
        P("tile", "rep", None, None),
        P("tile", "rep", None, None, None),
    )
    out_specs = (P("section", "tile", "rep", None), P("section", "tile", "rep", None))
    return jax.shard_map(shards, mesh=mesh, in_specs=in_specs, out_specs=out_specs, check_vma=False)
```

```python
import math

import jax
import jax.numpy as jnp
from jax import lax
from jax.sharding import PartitionSpec as P

HALO = 128


dead_time = 0.1
background = 0.1
loss_weight = 0.1
fresnel = 0.5
highest = lax.Precision.HIGHEST


def from_behind(value, axis, by):
    peers = lax.axis_size(axis)
    pairs = [(i, i + by) for i in range(peers) if 0 <= i + by < peers]
    return lax.ppermute(value, axis, pairs)


def left_product(matrix, frames):
    return jnp.einsum(
        "mk,bkn->bmn", matrix, frames, precision=highest, preferred_element_type=jnp.float32
    )


def right_product(frames, matrix):
    return jnp.einsum(
        "bmk,kn->bmn", frames, matrix, precision=highest, preferred_element_type=jnp.float32
    )


def sandwich(table_re, table_im, wave_re, wave_im):
    first_re = left_product(table_re, wave_re) - left_product(table_im, wave_im)
    first_im = left_product(table_re, wave_im) + left_product(table_im, wave_re)
    out_re = right_product(first_re, table_re) - right_product(first_im, table_im)
    out_im = right_product(first_re, table_im) + right_product(first_im, table_re)
    return (out_re, out_im)


def dft_tables(length):
    indices = jnp.arange(length, dtype=jnp.int32)
    product = indices[:, None] * indices[None, :] % length
    angles = product.astype(jnp.float32) * (2.0 * math.pi / length)
    cosine_table = jnp.cos(angles)
    sine_table = jnp.sin(angles)
    shifted = jnp.where(indices < length // 2, indices, indices - length).astype(jnp.float32)
    kernel = math.pi * fresnel * shifted * shifted / length

    def spread(weights):
        first_part = jnp.dot(cosine_table * weights[None, :], cosine_table, precision=highest)
        second_part = jnp.dot(sine_table * weights[None, :], sine_table, precision=highest)
        return (first_part + second_part) / length

    near_table = (spread(jnp.cos(kernel)), spread(jnp.sin(kernel)))
    norm_scale = 1.0 / math.sqrt(length)
    far_table = (cosine_table * norm_scale, -sine_table * norm_scale)
    return (near_table, far_table)


def block_tables(table_re, table_im):
    left = jnp.stack([jnp.stack([table_re, -table_im]), jnp.stack([table_im, table_re])])
    right = jnp.stack([jnp.stack([table_re, table_im]), jnp.stack([-table_im, table_re])])
    return (left, right)


def stacked_sandwich(pair, wave_re, wave_im):
    left, right = pair
    wave = jnp.stack([wave_re, wave_im])
    first = jnp.einsum("abmk,bkn->amn", left, wave, precision=lax.Precision.HIGH, preferred_element_type=jnp.float32)
    out = jnp.einsum("bmk,bakn->amn", first, right, precision=lax.Precision.HIGH, preferred_element_type=jnp.float32)
    return (out[0], out[1])


def place(block, offset, total, axis):
    reach = total - block.shape[axis]
    widths = [(0, 0)] * block.ndim
    widths[axis] = (reach, reach)
    return lax.dynamic_slice_in_dim(jnp.pad(block, widths), reach - offset, total, axis=axis)


def likelihood_seed(far_re, far_im, observed):
    intensity = far_re * far_re + far_im * far_im
    shifted_total = intensity + background
    denominator = 1.0 + dead_time * shifted_total
    model_rate = shifted_total / denominator
    slope_term = loss_weight * (1.0 - observed / model_rate) / (denominator * denominator)
    return (2.0 * slope_term * far_re, 2.0 * slope_term * far_im)


def shards(phase_shift, absorption, probe_wave, positions, counts):
    slices_here = phase_shift.shape[0]
    tile_width = phase_shift.shape[2]
    frame_width = probe_wave.shape[1]
    sections = lax.axis_size("section")
    tile_count = lax.axis_size("tile")
    grid_side = math.isqrt(tile_count)
    margin = HALO
    extent = tile_width + 2 * margin
    section_index = lax.axis_index("section")
    column = lax.axis_index("tile") % grid_side
    has_left = (column > 0).astype(jnp.float32)
    has_right = (column < grid_side - 1).astype(jnp.float32)
    own_block = jnp.stack([phase_shift[:, 0], absorption[:, 0]])

    low, high = tile_width - margin, margin
    slices_total = sections * slices_here
    corner = positions[0, 0, 0]
    corner_above = from_behind(corner, "tile", grid_side)
    corner_below = from_behind(corner, "tile", -grid_side)
    to_left = from_behind(own_block[:, :, :, low:], "tile", 1) * has_left
    to_right = from_behind(own_block[:, :, :, :high], "tile", -1) * has_right
    wide = jnp.concatenate([to_left, own_block, to_right], axis=3)
    band_down = lax.dynamic_slice_in_dim(wide[:, :, low:], corner_below[1], frame_width, axis=3)
    band_up = lax.dynamic_slice_in_dim(wide[:, :, :high], corner_above[1], frame_width, axis=3)
    above = from_behind(band_down, "tile", grid_side)
    below = from_behind(band_up, "tile", -grid_side)
    column_band = jnp.concatenate(
        [above, lax.dynamic_slice_in_dim(wide, corner[1], frame_width, axis=3), below], axis=2
    )
    window = lax.dynamic_slice_in_dim(column_band, corner[0], frame_width, axis=2)
    damping = jnp.exp(-window[1])
    own_objects = jnp.stack([damping * jnp.cos(window[0]), damping * jnp.sin(window[0])], axis=1)
    all_objects = lax.all_gather(own_objects, "section", axis=0, tiled=True)
    near_table, far_table = lax.optimization_barrier(dft_tables(frame_width))
    near_pair = block_tables(*near_table)
    far_pair = block_tables(*far_table)
    near_back = block_tables(near_table[0], -near_table[1])
    far_back = block_tables(far_table[0], -far_table[1])
    observed = counts[0, 0, 0].astype(jnp.float32)
    wave_re, wave_im = probe_wave[0], probe_wave[1]
    exits = []
    for slice_no in range(slices_total):
        object_re = all_objects[slice_no, 0]
        object_im = all_objects[slice_no, 1]
        exit_re = object_re * wave_re - object_im * wave_im
        exit_im = object_re * wave_im + object_im * wave_re
        exits.append((exit_re, exit_im))
        pair = near_pair if slice_no < slices_total - 1 else far_pair
        wave_re, wave_im = stacked_sandwich(pair, exit_re, exit_im)
    grad_re, grad_im = likelihood_seed(wave_re, wave_im, observed)
    terms = []
    for slice_no in reversed(range(slices_total)):
        pair = near_back if slice_no < slices_total - 1 else far_back
        back_re, back_im = stacked_sandwich(pair, grad_re, grad_im)
        exit_re, exit_im = exits[slice_no]
        phase_term = back_im * exit_re - back_re * exit_im
        absorb_term = -(back_re * exit_re + back_im * exit_im)
        terms.append(jnp.stack([phase_term, absorb_term]))
        if slice_no > 0:
            object_re = all_objects[slice_no, 0]
            object_im = all_objects[slice_no, 1]
            grad_re = object_re * back_re + object_im * back_im
            grad_im = object_re * back_im - object_im * back_re
    terms = jnp.stack(terms[::-1], axis=1)
    own_terms = lax.dynamic_slice_in_dim(terms, section_index * slices_here, slices_here, axis=1)
    grad_band = place(own_terms, corner[0], extent, axis=2)
    from_below = from_behind(grad_band[:, :, :margin], "tile", -grid_side)
    from_above = from_behind(grad_band[:, :, margin + tile_width :], "tile", grid_side)
    grad_wide = place(grad_band[:, :, margin : margin + tile_width], corner[1], extent, axis=3)
    grad_wide = grad_wide.at[:, :, low:].add(place(from_below, corner_below[1], extent, axis=3))
    grad_wide = grad_wide.at[:, :, :high].add(place(from_above, corner_above[1], extent, axis=3))
    middle = grad_wide[..., margin : margin + tile_width]
    from_right = from_behind(grad_wide[..., :margin], "tile", -1) * has_right
    from_left = from_behind(grad_wide[..., margin + tile_width :], "tile", 1) * has_left
    middle = middle.at[..., low:].add(from_right)
    middle = middle.at[..., :high].add(from_left)
    half = tile_width // 2
    rep_index = lax.axis_index("rep")
    kept = lax.dynamic_slice_in_dim(middle, rep_index * half, half, axis=2)
    sent = lax.dynamic_slice_in_dim(middle, (1 - rep_index) * half, half, axis=2)
    shares = kept + lax.ppermute(sent, "rep", [(0, 1), (1, 0)])
    return (shares[0][:, None], shares[1][:, None])


def solution(mesh):
    in_specs = (
        P("section", "tile", None, None),
        P("section", "tile", None, None),
        P(),
        P("tile", "rep", None, None),
        P("tile", "rep", None, None, None),
    )
    out_specs = (P("section", "tile", "rep", None), P("section", "tile", "rep", None))
    return jax.shard_map(shards, mesh=mesh, in_specs=in_specs, out_specs=out_specs, check_vma=False)
```

```python
import functools
import math

import jax
import jax.numpy as jnp
from jax import lax
from jax.experimental import pallas as pl
from jax.experimental.pallas import tpu as pltpu
from jax.sharding import PartitionSpec as P

MESH = pl.DeviceIdType.MESH

HALO = 128


dead_time = 0.1
background = 0.1
loss_weight = 0.1
fresnel = 0.5
highest = lax.Precision.HIGHEST


def from_behind(value, axis, by):
    peers = lax.axis_size(axis)
    pairs = [(i, i + by) for i in range(peers) if 0 <= i + by < peers]
    return lax.ppermute(value, axis, pairs)


def left_product(matrix, frames):
    return jnp.einsum(
        "mk,bkn->bmn", matrix, frames, precision=highest, preferred_element_type=jnp.float32
    )


def right_product(frames, matrix):
    return jnp.einsum(
        "bmk,kn->bmn", frames, matrix, precision=highest, preferred_element_type=jnp.float32
    )


def sandwich(table_re, table_im, wave_re, wave_im):
    first_re = left_product(table_re, wave_re) - left_product(table_im, wave_im)
    first_im = left_product(table_re, wave_im) + left_product(table_im, wave_re)
    out_re = right_product(first_re, table_re) - right_product(first_im, table_im)
    out_im = right_product(first_re, table_im) + right_product(first_im, table_re)
    return (out_re, out_im)


def dft_tables(length):
    indices = jnp.arange(length, dtype=jnp.int32)
    product = indices[:, None] * indices[None, :] % length
    angles = product.astype(jnp.float32) * (2.0 * math.pi / length)
    cosine_table = jnp.cos(angles)
    sine_table = jnp.sin(angles)
    shifted = jnp.where(indices < length // 2, indices, indices - length).astype(jnp.float32)
    kernel = math.pi * fresnel * shifted * shifted / length

    def spread(weights):
        first_part = jnp.dot(cosine_table * weights[None, :], cosine_table, precision=highest)
        second_part = jnp.dot(sine_table * weights[None, :], sine_table, precision=highest)
        return (first_part + second_part) / length

    near_table = (spread(jnp.cos(kernel)), spread(jnp.sin(kernel)))
    norm_scale = 1.0 / math.sqrt(length)
    far_table = (cosine_table * norm_scale, -sine_table * norm_scale)
    return (near_table, far_table)


def block_tables(table_re, table_im):
    left = jnp.stack([jnp.stack([table_re, -table_im]), jnp.stack([table_im, table_re])])
    right = jnp.stack([jnp.stack([table_re, table_im]), jnp.stack([-table_im, table_re])])
    return (left, right)


def stacked_sandwich(pair, wave_re, wave_im):
    left, right = pair
    wave = jnp.stack([wave_re, wave_im])
    first = jnp.einsum("abmk,bkn->amn", left, wave, precision=lax.Precision.HIGH, preferred_element_type=jnp.float32)
    out = jnp.einsum("bmk,bakn->amn", first, right, precision=lax.Precision.HIGH, preferred_element_type=jnp.float32)
    return (out[0], out[1])


def exchange_kernel(peers, own_ref, out_ref, held, send_sem, recv_sem):
    me = lax.axis_index("section")
    tile = lax.axis_index("tile")
    rep = lax.axis_index("rep")
    barrier = pltpu.get_barrier_semaphore()
    for shift in range(1, peers):
        pl.semaphore_signal(
            barrier, inc=1, device_id=(lax.rem(me + shift, peers), tile, rep), device_id_type=MESH
        )
    pl.semaphore_wait(barrier, peers - 1)
    copies = []
    for shift in range(1, peers):
        copy = pltpu.make_async_remote_copy(
            src_ref=own_ref,
            dst_ref=held.at[shift - 1],
            send_sem=send_sem.at[shift - 1],
            recv_sem=recv_sem.at[shift - 1],
            device_id=(lax.rem(me + peers - shift, peers), tile, rep),
            device_id_type=MESH,
        )
        copy.start()
        copies.append(copy)
    for copy in copies:
        copy.wait()
    out_ref[...] = held[...]


def gather_slices(own, sections):
    received = pl.pallas_call(
        functools.partial(exchange_kernel, sections),
        out_shape=jax.ShapeDtypeStruct((sections - 1,) + own.shape, own.dtype),
        in_specs=[pl.BlockSpec(memory_space=pltpu.VMEM)],
        out_specs=pl.BlockSpec(memory_space=pltpu.VMEM),
        scratch_shapes=[
            pltpu.VMEM((sections - 1,) + own.shape, own.dtype),
            pltpu.SemaphoreType.DMA((sections - 1,)),
            pltpu.SemaphoreType.DMA((sections - 1,)),
        ],
        compiler_params=pltpu.CompilerParams(collective_id=0, has_side_effects=True),
    )(own)
    got = [own] + [received[shift - 1] for shift in range(1, sections)]
    here = lax.axis_index("section")
    ordered = []
    for wanted in range(sections):
        pick = got[0]
        for shift in range(1, sections):
            pick = jnp.where((here + shift) % sections == wanted, got[shift], pick)
        ordered.append(pick)
    return jnp.concatenate(ordered, axis=0)


def place(block, offset, total, axis):
    reach = total - block.shape[axis]
    widths = [(0, 0)] * block.ndim
    widths[axis] = (reach, reach)
    return lax.dynamic_slice_in_dim(jnp.pad(block, widths), reach - offset, total, axis=axis)


def likelihood_seed(far_re, far_im, observed):
    intensity = far_re * far_re + far_im * far_im
    shifted_total = intensity + background
    denominator = 1.0 + dead_time * shifted_total
    model_rate = shifted_total / denominator
    slope_term = loss_weight * (1.0 - observed / model_rate) / (denominator * denominator)
    return (2.0 * slope_term * far_re, 2.0 * slope_term * far_im)


def shards(phase_shift, absorption, probe_wave, positions, counts):
    slices_here = phase_shift.shape[0]
    tile_width = phase_shift.shape[2]
    frame_width = probe_wave.shape[1]
    sections = lax.axis_size("section")
    tile_count = lax.axis_size("tile")
    grid_side = math.isqrt(tile_count)
    margin = HALO
    extent = tile_width + 2 * margin
    section_index = lax.axis_index("section")
    column = lax.axis_index("tile") % grid_side
    has_left = (column > 0).astype(jnp.float32)
    has_right = (column < grid_side - 1).astype(jnp.float32)
    own_block = jnp.stack([phase_shift[:, 0], absorption[:, 0]])

    low, high = tile_width - margin, margin
    slices_total = sections * slices_here
    corner = positions[0, 0, 0]
    corner_above = from_behind(corner, "tile", grid_side)
    corner_below = from_behind(corner, "tile", -grid_side)
    to_left = from_behind(own_block[:, :, :, low:], "tile", 1) * has_left
    to_right = from_behind(own_block[:, :, :, :high], "tile", -1) * has_right
    wide = jnp.concatenate([to_left, own_block, to_right], axis=3)
    band_down = lax.dynamic_slice_in_dim(wide[:, :, low:], corner_below[1], frame_width, axis=3)
    band_up = lax.dynamic_slice_in_dim(wide[:, :, :high], corner_above[1], frame_width, axis=3)
    above = from_behind(band_down, "tile", grid_side)
    below = from_behind(band_up, "tile", -grid_side)
    column_band = jnp.concatenate(
        [above, lax.dynamic_slice_in_dim(wide, corner[1], frame_width, axis=3), below], axis=2
    )
    window = lax.dynamic_slice_in_dim(column_band, corner[0], frame_width, axis=2)
    damping = jnp.exp(-window[1])
    own_objects = jnp.stack([damping * jnp.cos(window[0]), damping * jnp.sin(window[0])], axis=1)
    all_objects = gather_slices(own_objects, sections)
    near_table, far_table = lax.optimization_barrier(dft_tables(frame_width))
    near_pair = block_tables(*near_table)
    far_pair = block_tables(*far_table)
    near_back = block_tables(near_table[0], -near_table[1])
    far_back = block_tables(far_table[0], -far_table[1])
    observed = counts[0, 0, 0].astype(jnp.float32)
    wave_re, wave_im = probe_wave[0], probe_wave[1]
    exits = []
    for slice_no in range(slices_total):
        object_re = all_objects[slice_no, 0]
        object_im = all_objects[slice_no, 1]
        exit_re = object_re * wave_re - object_im * wave_im
        exit_im = object_re * wave_im + object_im * wave_re
        exits.append((exit_re, exit_im))
        pair = near_pair if slice_no < slices_total - 1 else far_pair
        wave_re, wave_im = stacked_sandwich(pair, exit_re, exit_im)
    grad_re, grad_im = likelihood_seed(wave_re, wave_im, observed)
    terms = []
    for slice_no in reversed(range(slices_total)):
        pair = near_back if slice_no < slices_total - 1 else far_back
        back_re, back_im = stacked_sandwich(pair, grad_re, grad_im)
        exit_re, exit_im = exits[slice_no]
        phase_term = back_im * exit_re - back_re * exit_im
        absorb_term = -(back_re * exit_re + back_im * exit_im)
        terms.append(jnp.stack([phase_term, absorb_term]))
        if slice_no > 0:
            object_re = all_objects[slice_no, 0]
            object_im = all_objects[slice_no, 1]
            grad_re = object_re * back_re + object_im * back_im
            grad_im = object_re * back_im - object_im * back_re
    terms = jnp.stack(terms[::-1], axis=1)
    own_terms = lax.dynamic_slice_in_dim(terms, section_index * slices_here, slices_here, axis=1)
    grad_band = place(own_terms, corner[0], extent, axis=2)
    from_below = from_behind(grad_band[:, :, :margin], "tile", -grid_side)
    from_above = from_behind(grad_band[:, :, margin + tile_width :], "tile", grid_side)
    grad_wide = place(grad_band[:, :, margin : margin + tile_width], corner[1], extent, axis=3)
    grad_wide = grad_wide.at[:, :, low:].add(place(from_below, corner_below[1], extent, axis=3))
    grad_wide = grad_wide.at[:, :, :high].add(place(from_above, corner_above[1], extent, axis=3))
    middle = grad_wide[..., margin : margin + tile_width]
    from_right = from_behind(grad_wide[..., :margin], "tile", -1) * has_right
    from_left = from_behind(grad_wide[..., margin + tile_width :], "tile", 1) * has_left
    middle = middle.at[..., low:].add(from_right)
    middle = middle.at[..., :high].add(from_left)
    half = tile_width // 2
    rep_index = lax.axis_index("rep")
    kept = lax.dynamic_slice_in_dim(middle, rep_index * half, half, axis=2)
    sent = lax.dynamic_slice_in_dim(middle, (1 - rep_index) * half, half, axis=2)
    shares = kept + lax.ppermute(sent, "rep", [(0, 1), (1, 0)])
    return (shares[0][:, None], shares[1][:, None])


def solution(mesh):
    in_specs = (
        P("section", "tile", None, None),
        P("section", "tile", None, None),
        P(),
        P("tile", "rep", None, None),
        P("tile", "rep", None, None, None),
    )
    out_specs = (P("section", "tile", "rep", None), P("section", "tile", "rep", None))
    return jax.shard_map(shards, mesh=mesh, in_specs=in_specs, out_specs=out_specs, check_vma=False)
```

```python
import math

import jax
import jax.numpy as jnp
from jax import lax
from jax.sharding import PartitionSpec as P

HALO = 128


dead_time = 0.1
background = 0.1
loss_weight = 0.1
fresnel = 0.5
highest = lax.Precision.HIGHEST


def from_behind(value, axis, by):
    peers = lax.axis_size(axis)
    pairs = [(i, i + by) for i in range(peers) if 0 <= i + by < peers]
    return lax.ppermute(value, axis, pairs)


def left_product(matrix, frames):
    return jnp.einsum(
        "mk,bkn->bmn", matrix, frames, precision=highest, preferred_element_type=jnp.float32
    )


def right_product(frames, matrix):
    return jnp.einsum(
        "bmk,kn->bmn", frames, matrix, precision=highest, preferred_element_type=jnp.float32
    )


def sandwich(table_re, table_im, wave_re, wave_im):
    first_re = left_product(table_re, wave_re) - left_product(table_im, wave_im)
    first_im = left_product(table_re, wave_im) + left_product(table_im, wave_re)
    out_re = right_product(first_re, table_re) - right_product(first_im, table_im)
    out_im = right_product(first_re, table_im) + right_product(first_im, table_re)
    return (out_re, out_im)


def dft_tables(length):
    indices = jnp.arange(length, dtype=jnp.int32)
    product = indices[:, None] * indices[None, :] % length
    angles = product.astype(jnp.float32) * (2.0 * math.pi / length)
    cosine_table = jnp.cos(angles)
    sine_table = jnp.sin(angles)
    shifted = jnp.where(indices < length // 2, indices, indices - length).astype(jnp.float32)
    kernel = math.pi * fresnel * shifted * shifted / length

    def spread(weights):
        first_part = jnp.dot(cosine_table * weights[None, :], cosine_table, precision=highest)
        second_part = jnp.dot(sine_table * weights[None, :], sine_table, precision=highest)
        return (first_part + second_part) / length

    near_table = (spread(jnp.cos(kernel)), spread(jnp.sin(kernel)))
    norm_scale = 1.0 / math.sqrt(length)
    far_table = (cosine_table * norm_scale, -sine_table * norm_scale)
    return (near_table, far_table)


def block_tables(table_re, table_im):
    left = jnp.stack([jnp.stack([table_re, -table_im]), jnp.stack([table_im, table_re])])
    right = jnp.stack([jnp.stack([table_re, table_im]), jnp.stack([-table_im, table_re])])
    return (left, right)


def stacked_sandwich(pair, wave_re, wave_im):
    left, right = pair
    wave = jnp.stack([wave_re, wave_im])
    first = jnp.einsum("abmk,bkn->amn", left, wave, precision=lax.Precision.HIGH, preferred_element_type=jnp.float32)
    out = jnp.einsum("bmk,bakn->amn", first, right, precision=lax.Precision.HIGH, preferred_element_type=jnp.float32)
    return (out[0], out[1])


def place(block, offset, total, axis):
    reach = total - block.shape[axis]
    widths = [(0, 0)] * block.ndim
    widths[axis] = (reach, reach)
    return lax.dynamic_slice_in_dim(jnp.pad(block, widths), reach - offset, total, axis=axis)


def likelihood_seed(far_re, far_im, observed):
    intensity = far_re * far_re + far_im * far_im
    shifted_total = intensity + background
    denominator = 1.0 + dead_time * shifted_total
    model_rate = shifted_total / denominator
    slope_term = loss_weight * (1.0 - observed / model_rate) / (denominator * denominator)
    return (2.0 * slope_term * far_re, 2.0 * slope_term * far_im)


def shards(phase_shift, absorption, probe_wave, positions, counts):
    slices_here = phase_shift.shape[0]
    tile_width = phase_shift.shape[2]
    frame_width = probe_wave.shape[1]
    sections = lax.axis_size("section")
    tile_count = lax.axis_size("tile")
    grid_side = math.isqrt(tile_count)
    margin = HALO
    extent = tile_width + 2 * margin
    section_index = lax.axis_index("section")
    column = lax.axis_index("tile") % grid_side
    has_left = (column > 0).astype(jnp.float32)
    has_right = (column < grid_side - 1).astype(jnp.float32)
    own_block = jnp.stack([phase_shift[:, 0], absorption[:, 0]])

    low, high = tile_width - margin, margin
    slices_total = sections * slices_here
    corner = positions[0, 0, 0]
    corner_above = from_behind(corner, "tile", grid_side)
    corner_below = from_behind(corner, "tile", -grid_side)
    to_left = from_behind(own_block[:, :, :, low:], "tile", 1) * has_left
    to_right = from_behind(own_block[:, :, :, :high], "tile", -1) * has_right
    wide = jnp.concatenate([to_left, own_block, to_right], axis=3)
    band_down = lax.dynamic_slice_in_dim(wide[:, :, low:], corner_below[1], frame_width, axis=3)
    band_up = lax.dynamic_slice_in_dim(wide[:, :, :high], corner_above[1], frame_width, axis=3)
    above = from_behind(band_down, "tile", grid_side)
    below = from_behind(band_up, "tile", -grid_side)
    column_band = jnp.concatenate(
        [above, lax.dynamic_slice_in_dim(wide, corner[1], frame_width, axis=3), below], axis=2
    )
    window = lax.dynamic_slice_in_dim(column_band, corner[0], frame_width, axis=2)
    damping = jnp.exp(-window[1])
    own_objects = jnp.stack([damping * jnp.cos(window[0]), damping * jnp.sin(window[0])], axis=1)
    all_objects = lax.all_gather(own_objects, "section", axis=0, tiled=True)
    near_table, far_table = lax.optimization_barrier(dft_tables(frame_width))
    near_pair = block_tables(*near_table)
    far_pair = block_tables(*far_table)
    near_back = block_tables(near_table[0], -near_table[1])
    far_back = block_tables(far_table[0], -far_table[1])
    observed = counts[0, 0, 0].astype(jnp.float32)
    wave_re, wave_im = probe_wave[0], probe_wave[1]
    exits = []
    for slice_no in range(slices_total):
        object_re = all_objects[slice_no, 0]
        object_im = all_objects[slice_no, 1]
        exit_re = object_re * wave_re - object_im * wave_im
        exit_im = object_re * wave_im + object_im * wave_re
        exits.append((exit_re, exit_im))
        pair = near_pair if slice_no < slices_total - 1 else far_pair
        wave_re, wave_im = stacked_sandwich(pair, exit_re, exit_im)
    grad_re, grad_im = likelihood_seed(wave_re, wave_im, observed)
    terms = []
    for slice_no in reversed(range(slices_total)):
        pair = near_back if slice_no < slices_total - 1 else far_back
        back_re, back_im = stacked_sandwich(pair, grad_re, grad_im)
        exit_re, exit_im = exits[slice_no]
        phase_term = back_im * exit_re - back_re * exit_im
        absorb_term = -(back_re * exit_re + back_im * exit_im)
        terms.append(jnp.stack([phase_term, absorb_term]))
        if slice_no > 0:
            object_re = all_objects[slice_no, 0]
            object_im = all_objects[slice_no, 1]
            grad_re = object_re * back_re + object_im * back_im
            grad_im = object_re * back_im - object_im * back_re
    terms = jnp.stack(terms[::-1], axis=1)
    own_terms = lax.dynamic_slice_in_dim(terms, section_index * slices_here, slices_here, axis=1)
    grad_band = place(own_terms, corner[0], extent, axis=2)
    from_below = from_behind(grad_band[:, :, :margin], "tile", -grid_side)
    from_above = from_behind(grad_band[:, :, margin + tile_width :], "tile", grid_side)
    grad_wide = place(grad_band[:, :, margin : margin + tile_width], corner[1], extent, axis=3)
    grad_wide = grad_wide.at[:, :, low:].add(place(from_below, corner_below[1], extent, axis=3))
    grad_wide = grad_wide.at[:, :, :high].add(place(from_above, corner_above[1], extent, axis=3))
    half = tile_width // 2
    reps = lax.axis_size("rep")
    rep_index = lax.axis_index("rep")

    def rows_of(block, which):
        return lax.dynamic_slice_in_dim(block, which * half, half, axis=2)

    def to_tile(block, shift, cross):
        pairs = []
        for tile in range(tile_count):
            if 0 <= tile + shift < tile_count:
                for rep in range(reps):
                    pairs.append((tile * reps + rep, (tile + shift) * reps + (reps - 1 - rep if cross else rep)))
        return lax.ppermute(block, ("tile", "rep"), pairs)

    left_strip = grad_wide[..., :margin]
    right_strip = grad_wide[..., margin + tile_width :]
    from_right = to_tile(rows_of(left_strip, rep_index), -1, False) + to_tile(
        rows_of(left_strip, 1 - rep_index), -1, True
    )
    from_left = to_tile(rows_of(right_strip, rep_index), 1, False) + to_tile(
        rows_of(right_strip, 1 - rep_index), 1, True
    )
    middle = grad_wide[..., margin : margin + tile_width]
    kept = rows_of(middle, rep_index)
    shares = kept + lax.ppermute(rows_of(middle, 1 - rep_index), "rep", [(0, 1), (1, 0)])
    shares = shares.at[..., low:].add(from_right * has_right)
    shares = shares.at[..., :high].add(from_left * has_left)
    return (shares[0][:, None], shares[1][:, None])

def solution(mesh):
    in_specs = (
        P("section", "tile", None, None),
        P("section", "tile", None, None),
        P(),
        P("tile", "rep", None, None),
        P("tile", "rep", None, None, None),
    )
    out_specs = (P("section", "tile", "rep", None), P("section", "tile", "rep", None))
    return jax.shard_map(shards, mesh=mesh, in_specs=in_specs, out_specs=out_specs, check_vma=False)
```

```python
import math

import jax
import jax.numpy as jnp
from jax import lax
from jax.sharding import PartitionSpec as P

HALO = 128


dead_time = 0.1
background = 0.1
loss_weight = 0.1
fresnel = 0.5
highest = lax.Precision.HIGHEST


def from_behind(value, axis, by):
    peers = lax.axis_size(axis)
    pairs = [(i, i + by) for i in range(peers) if 0 <= i + by < peers]
    return lax.ppermute(value, axis, pairs)


def left_product(matrix, frames):
    return jnp.einsum(
        "mk,bkn->bmn", matrix, frames, precision=highest, preferred_element_type=jnp.float32
    )


def right_product(frames, matrix):
    return jnp.einsum(
        "bmk,kn->bmn", frames, matrix, precision=highest, preferred_element_type=jnp.float32
    )


def sandwich(table_re, table_im, wave_re, wave_im):
    first_re = left_product(table_re, wave_re) - left_product(table_im, wave_im)
    first_im = left_product(table_re, wave_im) + left_product(table_im, wave_re)
    out_re = right_product(first_re, table_re) - right_product(first_im, table_im)
    out_im = right_product(first_re, table_im) + right_product(first_im, table_re)
    return (out_re, out_im)


def dft_tables(length):
    indices = jnp.arange(length, dtype=jnp.int32)
    product = indices[:, None] * indices[None, :] % length
    angles = product.astype(jnp.float32) * (2.0 * math.pi / length)
    cosine_table = jnp.cos(angles)
    sine_table = jnp.sin(angles)
    shifted = jnp.where(indices < length // 2, indices, indices - length).astype(jnp.float32)
    kernel = math.pi * fresnel * shifted * shifted / length

    def spread(weights):
        first_part = jnp.dot(cosine_table * weights[None, :], cosine_table, precision=highest)
        second_part = jnp.dot(sine_table * weights[None, :], sine_table, precision=highest)
        return (first_part + second_part) / length

    near_table = (spread(jnp.cos(kernel)), spread(jnp.sin(kernel)))
    norm_scale = 1.0 / math.sqrt(length)
    far_table = (cosine_table * norm_scale, -sine_table * norm_scale)
    return (near_table, far_table)


def block_tables(table_re, table_im):
    left = jnp.stack([jnp.stack([table_re, -table_im]), jnp.stack([table_im, table_re])])
    right = jnp.stack([jnp.stack([table_re, table_im]), jnp.stack([-table_im, table_re])])
    return (left, right)


def stacked_sandwich(pair, wave_re, wave_im):
    left, right = pair
    wave = jnp.stack([wave_re, wave_im])
    first = jnp.einsum("abmk,bkn->amn", left, wave, precision=lax.Precision.HIGH, preferred_element_type=jnp.float32)
    out = jnp.einsum("bmk,bakn->amn", first, right, precision=lax.Precision.HIGH, preferred_element_type=jnp.float32)
    return (out[0], out[1])


def place(block, offset, total, axis):
    reach = total - block.shape[axis]
    widths = [(0, 0)] * block.ndim
    widths[axis] = (reach, reach)
    return lax.dynamic_slice_in_dim(jnp.pad(block, widths), reach - offset, total, axis=axis)


def likelihood_seed(far_re, far_im, observed):
    intensity = far_re * far_re + far_im * far_im
    shifted_total = intensity + background
    denominator = 1.0 + dead_time * shifted_total
    model_rate = shifted_total / denominator
    slope_term = loss_weight * (1.0 - observed / model_rate) / (denominator * denominator)
    return (2.0 * slope_term * far_re, 2.0 * slope_term * far_im)


def shards(phase_shift, absorption, probe_wave, positions, counts):
    slices_here = phase_shift.shape[0]
    tile_width = phase_shift.shape[2]
    frame_width = probe_wave.shape[1]
    sections = lax.axis_size("section")
    tile_count = lax.axis_size("tile")
    grid_side = math.isqrt(tile_count)
    margin = HALO
    extent = tile_width + 2 * margin
    section_index = lax.axis_index("section")
    column = lax.axis_index("tile") % grid_side
    has_left = (column > 0).astype(jnp.float32)
    has_right = (column < grid_side - 1).astype(jnp.float32)
    own_block = jnp.stack([phase_shift[:, 0], absorption[:, 0]])

    low, high = tile_width - margin, margin
    slices_total = sections * slices_here
    tile_here = lax.axis_index("tile")
    rep_here = lax.axis_index("rep")
    corner = positions[tile_here, rep_here, 0]
    corner_above = positions[(tile_here + tile_count - grid_side) % tile_count, rep_here, 0]
    corner_below = positions[(tile_here + grid_side) % tile_count, rep_here, 0]
    to_left = from_behind(own_block[:, :, :, low:], "tile", 1) * has_left
    to_right = from_behind(own_block[:, :, :, :high], "tile", -1) * has_right
    wide = jnp.concatenate([to_left, own_block, to_right], axis=3)
    band_down = lax.dynamic_slice_in_dim(wide[:, :, low:], corner_below[1], frame_width, axis=3)
    band_up = lax.dynamic_slice_in_dim(wide[:, :, :high], corner_above[1], frame_width, axis=3)
    above = from_behind(band_down, "tile", grid_side)
    below = from_behind(band_up, "tile", -grid_side)
    column_band = jnp.concatenate(
        [above, lax.dynamic_slice_in_dim(wide, corner[1], frame_width, axis=3), below], axis=2
    )
    window = lax.dynamic_slice_in_dim(column_band, corner[0], frame_width, axis=2)
    damping = jnp.exp(-window[1])
    own_objects = jnp.stack([damping * jnp.cos(window[0]), damping * jnp.sin(window[0])], axis=1)
    all_objects = lax.all_gather(own_objects, "section", axis=0, tiled=True)
    near_table, far_table = lax.optimization_barrier(dft_tables(frame_width))
    near_pair = block_tables(*near_table)
    far_pair = block_tables(*far_table)
    near_back = block_tables(near_table[0], -near_table[1])
    far_back = block_tables(far_table[0], -far_table[1])
    observed = counts[0, 0, 0].astype(jnp.float32)
    wave_re, wave_im = probe_wave[0], probe_wave[1]
    exits = []
    for slice_no in range(slices_total):
        object_re = all_objects[slice_no, 0]
        object_im = all_objects[slice_no, 1]
        exit_re = object_re * wave_re - object_im * wave_im
        exit_im = object_re * wave_im + object_im * wave_re
        exits.append((exit_re, exit_im))
        pair = near_pair if slice_no < slices_total - 1 else far_pair
        wave_re, wave_im = stacked_sandwich(pair, exit_re, exit_im)
    grad_re, grad_im = likelihood_seed(wave_re, wave_im, observed)
    terms = []
    for slice_no in reversed(range(slices_total)):
        pair = near_back if slice_no < slices_total - 1 else far_back
        back_re, back_im = stacked_sandwich(pair, grad_re, grad_im)
        exit_re, exit_im = exits[slice_no]
        phase_term = back_im * exit_re - back_re * exit_im
        absorb_term = -(back_re * exit_re + back_im * exit_im)
        terms.append(jnp.stack([phase_term, absorb_term]))
        if slice_no > 0:
            object_re = all_objects[slice_no, 0]
            object_im = all_objects[slice_no, 1]
            grad_re = object_re * back_re + object_im * back_im
            grad_im = object_re * back_im - object_im * back_re
    terms = jnp.stack(terms[::-1], axis=1)
    own_terms = lax.dynamic_slice_in_dim(terms, section_index * slices_here, slices_here, axis=1)
    grad_band = place(own_terms, corner[0], extent, axis=2)
    from_below = from_behind(grad_band[:, :, :margin], "tile", -grid_side)
    from_above = from_behind(grad_band[:, :, margin + tile_width :], "tile", grid_side)
    grad_wide = place(grad_band[:, :, margin : margin + tile_width], corner[1], extent, axis=3)
    grad_wide = grad_wide.at[:, :, low:].add(place(from_below, corner_below[1], extent, axis=3))
    grad_wide = grad_wide.at[:, :, :high].add(place(from_above, corner_above[1], extent, axis=3))
    half = tile_width // 2
    reps = lax.axis_size("rep")
    rep_index = lax.axis_index("rep")

    def rows_of(block, which):
        return lax.dynamic_slice_in_dim(block, which * half, half, axis=2)

    def to_tile(block, shift, cross):
        pairs = []
        for tile in range(tile_count):
            if 0 <= tile + shift < tile_count:
                for rep in range(reps):
                    pairs.append((tile * reps + rep, (tile + shift) * reps + (reps - 1 - rep if cross else rep)))
        return lax.ppermute(block, ("tile", "rep"), pairs)

    left_strip = grad_wide[..., :margin]
    right_strip = grad_wide[..., margin + tile_width :]
    from_right = to_tile(rows_of(left_strip, rep_index), -1, False) + to_tile(
        rows_of(left_strip, 1 - rep_index), -1, True
    )
    from_left = to_tile(rows_of(right_strip, rep_index), 1, False) + to_tile(
        rows_of(right_strip, 1 - rep_index), 1, True
    )
    middle = grad_wide[..., margin : margin + tile_width]
    kept = rows_of(middle, rep_index)
    shares = kept + lax.ppermute(rows_of(middle, 1 - rep_index), "rep", [(0, 1), (1, 0)])
    shares = shares.at[..., low:].add(from_right * has_right)
    shares = shares.at[..., :high].add(from_left * has_left)
    return (shares[0][:, None], shares[1][:, None])

def solution(mesh):
    in_specs = (
        P("section", "tile", None, None),
        P("section", "tile", None, None),
        P(),
        P(),
        P("tile", "rep", None, None, None),
    )
    out_specs = (P("section", "tile", "rep", None), P("section", "tile", "rep", None))
    return jax.shard_map(shards, mesh=mesh, in_specs=in_specs, out_specs=out_specs, check_vma=False)
```

```python
import functools
import math

import jax
import jax.numpy as jnp
from jax import lax
from jax.experimental import pallas as pl
from jax.experimental.pallas import tpu as pltpu
from jax.sharding import PartitionSpec as P

MESH = pl.DeviceIdType.MESH

HALO = 128


dead_time = 0.1
background = 0.1
loss_weight = 0.1
fresnel = 0.5
highest = lax.Precision.HIGHEST


def from_behind(value, axis, by):
    peers = lax.axis_size(axis)
    pairs = [(i, i + by) for i in range(peers) if 0 <= i + by < peers]
    return lax.ppermute(value, axis, pairs)


def left_product(matrix, frames):
    return jnp.einsum(
        "mk,bkn->bmn", matrix, frames, precision=highest, preferred_element_type=jnp.float32
    )


def right_product(frames, matrix):
    return jnp.einsum(
        "bmk,kn->bmn", frames, matrix, precision=highest, preferred_element_type=jnp.float32
    )


def sandwich(table_re, table_im, wave_re, wave_im):
    first_re = left_product(table_re, wave_re) - left_product(table_im, wave_im)
    first_im = left_product(table_re, wave_im) + left_product(table_im, wave_re)
    out_re = right_product(first_re, table_re) - right_product(first_im, table_im)
    out_im = right_product(first_re, table_im) + right_product(first_im, table_re)
    return (out_re, out_im)


def dft_tables(length):
    indices = jnp.arange(length, dtype=jnp.int32)
    product = indices[:, None] * indices[None, :] % length
    angles = product.astype(jnp.float32) * (2.0 * math.pi / length)
    cosine_table = jnp.cos(angles)
    sine_table = jnp.sin(angles)
    shifted = jnp.where(indices < length // 2, indices, indices - length).astype(jnp.float32)
    kernel = math.pi * fresnel * shifted * shifted / length

    def spread(weights):
        first_part = jnp.dot(cosine_table * weights[None, :], cosine_table, precision=highest)
        second_part = jnp.dot(sine_table * weights[None, :], sine_table, precision=highest)
        return (first_part + second_part) / length

    near_table = (spread(jnp.cos(kernel)), spread(jnp.sin(kernel)))
    norm_scale = 1.0 / math.sqrt(length)
    far_table = (cosine_table * norm_scale, -sine_table * norm_scale)
    return (near_table, far_table)


def block_tables(table_re, table_im):
    left = jnp.stack([jnp.stack([table_re, -table_im]), jnp.stack([table_im, table_re])])
    right = jnp.stack([jnp.stack([table_re, table_im]), jnp.stack([-table_im, table_re])])
    return (left, right)


def stacked_sandwich(pair, wave_re, wave_im):
    left, right = pair
    wave = jnp.stack([wave_re, wave_im])
    first = jnp.einsum("abmk,bkn->amn", left, wave, precision=lax.Precision.HIGH, preferred_element_type=jnp.float32)
    out = jnp.einsum("bmk,bakn->amn", first, right, precision=lax.Precision.HIGH, preferred_element_type=jnp.float32)
    return (out[0], out[1])


def exchange_kernel(peers, own_ref, out_ref, held, relay_up, relay_down, send_sem, recv_sem):
    me = lax.axis_index("section")
    tile = lax.axis_index("tile")
    rep = lax.axis_index("rep")
    ahead = (lax.rem(me + 1, peers), tile, rep)
    behind = (lax.rem(me + peers - 1, peers), tile, rep)
    rows = own_ref.shape[2] // 2
    barrier = pltpu.get_barrier_semaphore()
    for partner in (ahead, behind):
        pl.semaphore_signal(barrier, inc=1, device_id=partner, device_id_type=MESH)
    pl.semaphore_wait(barrier, 2)

    def remote(lane, src, dst, partner):
        copy = pltpu.make_async_remote_copy(
            src_ref=src,
            dst_ref=dst,
            send_sem=send_sem.at[lane],
            recv_sem=recv_sem.at[lane],
            device_id=partner,
            device_id_type=MESH,
        )
        copy.start()
        return copy

    first = [
        remote(0, own_ref, held.at[0], behind),
        remote(1, own_ref, held.at[2], ahead),
        remote(2, own_ref.at[:, :, :rows], relay_up, ahead),
        remote(3, own_ref.at[:, :, rows:], relay_down, behind),
    ]
    first[2].wait()
    first[3].wait()
    second = [
        remote(4, relay_up, held.at[1, :, :, :rows], ahead),
        remote(5, relay_down, held.at[1, :, :, rows:], behind),
    ]
    for copy in first[:2] + second:
        copy.wait()
    out_ref[...] = held[...]


def gather_slices(own, sections):
    half = own.shape[:2] + (own.shape[2] // 2,) + own.shape[3:]
    received = pl.pallas_call(
        functools.partial(exchange_kernel, sections),
        out_shape=jax.ShapeDtypeStruct((sections - 1,) + own.shape, own.dtype),
        in_specs=[pl.BlockSpec(memory_space=pltpu.VMEM)],
        out_specs=pl.BlockSpec(memory_space=pltpu.VMEM),
        scratch_shapes=[
            pltpu.VMEM((sections - 1,) + own.shape, own.dtype),
            pltpu.VMEM(half, own.dtype),
            pltpu.VMEM(half, own.dtype),
            pltpu.SemaphoreType.DMA((6,)),
            pltpu.SemaphoreType.DMA((6,)),
        ],
        compiler_params=pltpu.CompilerParams(collective_id=0, has_side_effects=True),
    )(own)
    got = [own] + [received[shift - 1] for shift in range(1, sections)]
    here = lax.axis_index("section")
    ordered = []
    for wanted in range(sections):
        pick = got[0]
        for shift in range(1, sections):
            pick = jnp.where((here + shift) % sections == wanted, got[shift], pick)
        ordered.append(pick)
    return jnp.concatenate(ordered, axis=0)


def place(block, offset, total, axis):
    reach = total - block.shape[axis]
    widths = [(0, 0)] * block.ndim
    widths[axis] = (reach, reach)
    return lax.dynamic_slice_in_dim(jnp.pad(block, widths), reach - offset, total, axis=axis)


def likelihood_seed(far_re, far_im, observed):
    intensity = far_re * far_re + far_im * far_im
    shifted_total = intensity + background
    denominator = 1.0 + dead_time * shifted_total
    model_rate = shifted_total / denominator
    slope_term = loss_weight * (1.0 - observed / model_rate) / (denominator * denominator)
    return (2.0 * slope_term * far_re, 2.0 * slope_term * far_im)


def shards(phase_shift, absorption, probe_wave, positions, counts):
    slices_here = phase_shift.shape[0]
    tile_width = phase_shift.shape[2]
    frame_width = probe_wave.shape[1]
    sections = lax.axis_size("section")
    tile_count = lax.axis_size("tile")
    grid_side = math.isqrt(tile_count)
    margin = HALO
    extent = tile_width + 2 * margin
    section_index = lax.axis_index("section")
    column = lax.axis_index("tile") % grid_side
    has_left = (column > 0).astype(jnp.float32)
    has_right = (column < grid_side - 1).astype(jnp.float32)
    own_block = jnp.stack([phase_shift[:, 0], absorption[:, 0]])

    low, high = tile_width - margin, margin
    slices_total = sections * slices_here
    corner = positions[0, 0, 0]
    corner_above = from_behind(corner, "tile", grid_side)
    corner_below = from_behind(corner, "tile", -grid_side)
    to_left = from_behind(own_block[:, :, :, low:], "tile", 1) * has_left
    to_right = from_behind(own_block[:, :, :, :high], "tile", -1) * has_right
    wide = jnp.concatenate([to_left, own_block, to_right], axis=3)
    band_down = lax.dynamic_slice_in_dim(wide[:, :, low:], corner_below[1], frame_width, axis=3)
    band_up = lax.dynamic_slice_in_dim(wide[:, :, :high], corner_above[1], frame_width, axis=3)
    above = from_behind(band_down, "tile", grid_side)
    below = from_behind(band_up, "tile", -grid_side)
    column_band = jnp.concatenate(
        [above, lax.dynamic_slice_in_dim(wide, corner[1], frame_width, axis=3), below], axis=2
    )
    window = lax.dynamic_slice_in_dim(column_band, corner[0], frame_width, axis=2)
    damping = jnp.exp(-window[1])
    own_objects = jnp.stack([damping * jnp.cos(window[0]), damping * jnp.sin(window[0])], axis=1)
    all_objects = gather_slices(own_objects, sections)
    near_table, far_table = lax.optimization_barrier(dft_tables(frame_width))
    near_pair = block_tables(*near_table)
    far_pair = block_tables(*far_table)
    near_back = block_tables(near_table[0], -near_table[1])
    far_back = block_tables(far_table[0], -far_table[1])
    observed = counts[0, 0, 0].astype(jnp.float32)
    wave_re, wave_im = probe_wave[0], probe_wave[1]
    exits = []
    for slice_no in range(slices_total):
        object_re = all_objects[slice_no, 0]
        object_im = all_objects[slice_no, 1]
        exit_re = object_re * wave_re - object_im * wave_im
        exit_im = object_re * wave_im + object_im * wave_re
        exits.append((exit_re, exit_im))
        pair = near_pair if slice_no < slices_total - 1 else far_pair
        wave_re, wave_im = stacked_sandwich(pair, exit_re, exit_im)
    grad_re, grad_im = likelihood_seed(wave_re, wave_im, observed)
    terms = []
    for slice_no in reversed(range(slices_total)):
        pair = near_back if slice_no < slices_total - 1 else far_back
        back_re, back_im = stacked_sandwich(pair, grad_re, grad_im)
        exit_re, exit_im = exits[slice_no]
        phase_term = back_im * exit_re - back_re * exit_im
        absorb_term = -(back_re * exit_re + back_im * exit_im)
        terms.append(jnp.stack([phase_term, absorb_term]))
        if slice_no > 0:
            object_re = all_objects[slice_no, 0]
            object_im = all_objects[slice_no, 1]
            grad_re = object_re * back_re + object_im * back_im
            grad_im = object_re * back_im - object_im * back_re
    terms = jnp.stack(terms[::-1], axis=1)
    own_terms = lax.dynamic_slice_in_dim(terms, section_index * slices_here, slices_here, axis=1)
    grad_band = place(own_terms, corner[0], extent, axis=2)
    from_below = from_behind(grad_band[:, :, :margin], "tile", -grid_side)
    from_above = from_behind(grad_band[:, :, margin + tile_width :], "tile", grid_side)
    grad_wide = place(grad_band[:, :, margin : margin + tile_width], corner[1], extent, axis=3)
    grad_wide = grad_wide.at[:, :, low:].add(place(from_below, corner_below[1], extent, axis=3))
    grad_wide = grad_wide.at[:, :, :high].add(place(from_above, corner_above[1], extent, axis=3))
    half = tile_width // 2
    reps = lax.axis_size("rep")
    rep_index = lax.axis_index("rep")

    def rows_of(block, which):
        return lax.dynamic_slice_in_dim(block, which * half, half, axis=2)

    def to_tile(block, shift, cross):
        pairs = []
        for tile in range(tile_count):
            if 0 <= tile + shift < tile_count:
                for rep in range(reps):
                    pairs.append((tile * reps + rep, (tile + shift) * reps + (reps - 1 - rep if cross else rep)))
        return lax.ppermute(block, ("tile", "rep"), pairs)

    left_strip = grad_wide[..., :margin]
    right_strip = grad_wide[..., margin + tile_width :]
    from_right = to_tile(rows_of(left_strip, rep_index), -1, False) + to_tile(
        rows_of(left_strip, 1 - rep_index), -1, True
    )
    from_left = to_tile(rows_of(right_strip, rep_index), 1, False) + to_tile(
        rows_of(right_strip, 1 - rep_index), 1, True
    )
    middle = grad_wide[..., margin : margin + tile_width]
    kept = rows_of(middle, rep_index)
    shares = kept + lax.ppermute(rows_of(middle, 1 - rep_index), "rep", [(0, 1), (1, 0)])
    shares = shares.at[..., low:].add(from_right * has_right)
    shares = shares.at[..., :high].add(from_left * has_left)
    return (shares[0][:, None], shares[1][:, None])

def solution(mesh):
    in_specs = (
        P("section", "tile", None, None),
        P("section", "tile", None, None),
        P(),
        P("tile", "rep", None, None),
        P("tile", "rep", None, None, None),
    )
    out_specs = (P("section", "tile", "rep", None), P("section", "tile", "rep", None))
    return jax.shard_map(shards, mesh=mesh, in_specs=in_specs, out_specs=out_specs, check_vma=False)
```

```python
import math

import jax
import jax.numpy as jnp
from jax import lax
from jax.sharding import PartitionSpec as P

HALO = 128


dead_time = 0.1
background = 0.1
loss_weight = 0.1
fresnel = 0.5
highest = lax.Precision.HIGHEST


def from_behind(value, axis, by):
    peers = lax.axis_size(axis)
    pairs = [(i, i + by) for i in range(peers) if 0 <= i + by < peers]
    return lax.ppermute(value, axis, pairs)


def left_product(matrix, frames):
    return jnp.einsum(
        "mk,bkn->bmn", matrix, frames, precision=highest, preferred_element_type=jnp.float32
    )


def right_product(frames, matrix):
    return jnp.einsum(
        "bmk,kn->bmn", frames, matrix, precision=highest, preferred_element_type=jnp.float32
    )


def sandwich(table_re, table_im, wave_re, wave_im):
    first_re = left_product(table_re, wave_re) - left_product(table_im, wave_im)
    first_im = left_product(table_re, wave_im) + left_product(table_im, wave_re)
    out_re = right_product(first_re, table_re) - right_product(first_im, table_im)
    out_im = right_product(first_re, table_im) + right_product(first_im, table_re)
    return (out_re, out_im)


def dft_tables(length):
    indices = jnp.arange(length, dtype=jnp.int32)
    product = indices[:, None] * indices[None, :] % length
    angles = product.astype(jnp.float32) * (2.0 * math.pi / length)
    cosine_table = jnp.cos(angles)
    sine_table = jnp.sin(angles)
    shifted = jnp.where(indices < length // 2, indices, indices - length).astype(jnp.float32)
    kernel = math.pi * fresnel * shifted * shifted / length

    def spread(weights):
        first_part = jnp.dot(cosine_table * weights[None, :], cosine_table, precision=highest)
        second_part = jnp.dot(sine_table * weights[None, :], sine_table, precision=highest)
        return (first_part + second_part) / length

    near_table = (spread(jnp.cos(kernel)), spread(jnp.sin(kernel)))
    norm_scale = 1.0 / math.sqrt(length)
    far_table = (cosine_table * norm_scale, -sine_table * norm_scale)
    return (near_table, far_table)


def block_tables(table_re, table_im):
    left = jnp.stack([jnp.stack([table_re, -table_im]), jnp.stack([table_im, table_re])])
    right = jnp.stack([jnp.stack([table_re, table_im]), jnp.stack([-table_im, table_re])])
    return (left, right)


def stacked_sandwich(pair, wave_re, wave_im):
    left, right = pair
    wave = jnp.stack([wave_re, wave_im])
    first = jnp.einsum("abmk,bkn->amn", left, wave, precision=lax.Precision.HIGH, preferred_element_type=jnp.float32)
    out = jnp.einsum("bmk,bakn->amn", first, right, precision=lax.Precision.HIGH, preferred_element_type=jnp.float32)
    return (out[0], out[1])


def place(block, offset, total, axis):
    reach = total - block.shape[axis]
    widths = [(0, 0)] * block.ndim
    widths[axis] = (reach, reach)
    return lax.dynamic_slice_in_dim(jnp.pad(block, widths), reach - offset, total, axis=axis)


def likelihood_seed(far_re, far_im, observed):
    intensity = far_re * far_re + far_im * far_im
    shifted_total = intensity + background
    denominator = 1.0 + dead_time * shifted_total
    model_rate = shifted_total / denominator
    slope_term = loss_weight * (1.0 - observed / model_rate) / (denominator * denominator)
    return (2.0 * slope_term * far_re, 2.0 * slope_term * far_im)


def shards(phase_shift, absorption, probe_wave, positions, counts):
    slices_here = phase_shift.shape[0]
    tile_width = phase_shift.shape[2]
    frame_width = probe_wave.shape[1]
    sections = lax.axis_size("section")
    tile_count = lax.axis_size("tile")
    grid_side = math.isqrt(tile_count)
    margin = HALO
    extent = tile_width + 2 * margin
    section_index = lax.axis_index("section")
    column = lax.axis_index("tile") % grid_side
    has_left = (column > 0).astype(jnp.float32)
    has_right = (column < grid_side - 1).astype(jnp.float32)
    own_block = jnp.stack([phase_shift[:, 0], absorption[:, 0]])

    low, high = tile_width - margin, margin
    slices_total = sections * slices_here
    corner = positions[0, 0, 0]
    corner_above = from_behind(corner, "tile", grid_side)
    corner_below = from_behind(corner, "tile", -grid_side)
    to_left = from_behind(own_block[:, :, :, low:], "tile", 1) * has_left
    to_right = from_behind(own_block[:, :, :, :high], "tile", -1) * has_right
    wide = jnp.concatenate([to_left, own_block, to_right], axis=3)
    band_down = lax.dynamic_slice_in_dim(wide[:, :, low:], corner_below[1], frame_width, axis=3)
    band_up = lax.dynamic_slice_in_dim(wide[:, :, :high], corner_above[1], frame_width, axis=3)
    above = from_behind(band_down, "tile", grid_side)
    below = from_behind(band_up, "tile", -grid_side)
    middle_band = lax.dynamic_slice_in_dim(wide, corner[1], frame_width, axis=3)
    padded_middle = jnp.pad(middle_band, ((0, 0), (0, 0), (margin, margin), (0, 0)))
    early = lax.dynamic_slice_in_dim(padded_middle, corner[0], frame_width, axis=2)
    early_all = lax.all_gather(early, "section", axis=1, tiled=True)
    column_band = jnp.concatenate([above, middle_band, below], axis=2)
    window = lax.dynamic_slice_in_dim(column_band, corner[0], frame_width, axis=2)
    late_row = jnp.where(corner[0] < margin, 0, frame_width - margin)
    late = lax.dynamic_slice_in_dim(window, late_row, margin, axis=2)
    late_all = lax.all_gather(late, "section", axis=1, tiled=True)
    raw_all = lax.dynamic_update_slice_in_dim(early_all, late_all, late_row, axis=2)
    damping = jnp.exp(-raw_all[1])
    all_objects = jnp.stack([damping * jnp.cos(raw_all[0]), damping * jnp.sin(raw_all[0])], axis=1)
    near_table, far_table = lax.optimization_barrier(dft_tables(frame_width))
    near_pair = block_tables(*near_table)
    far_pair = block_tables(*far_table)
    near_back = block_tables(near_table[0], -near_table[1])
    far_back = block_tables(far_table[0], -far_table[1])
    observed = counts[0, 0, 0].astype(jnp.float32)
    wave_re, wave_im = probe_wave[0], probe_wave[1]
    exits = []
    for slice_no in range(slices_total):
        object_re = all_objects[slice_no, 0]
        object_im = all_objects[slice_no, 1]
        exit_re = object_re * wave_re - object_im * wave_im
        exit_im = object_re * wave_im + object_im * wave_re
        exits.append((exit_re, exit_im))
        pair = near_pair if slice_no < slices_total - 1 else far_pair
        wave_re, wave_im = stacked_sandwich(pair, exit_re, exit_im)
    grad_re, grad_im = likelihood_seed(wave_re, wave_im, observed)
    terms = []
    for slice_no in reversed(range(slices_total)):
        pair = near_back if slice_no < slices_total - 1 else far_back
        back_re, back_im = stacked_sandwich(pair, grad_re, grad_im)
        exit_re, exit_im = exits[slice_no]
        phase_term = back_im * exit_re - back_re * exit_im
        absorb_term = -(back_re * exit_re + back_im * exit_im)
        terms.append(jnp.stack([phase_term, absorb_term]))
        if slice_no > 0:
            object_re = all_objects[slice_no, 0]
            object_im = all_objects[slice_no, 1]
            grad_re = object_re * back_re + object_im * back_im
            grad_im = object_re * back_im - object_im * back_re
    terms = jnp.stack(terms[::-1], axis=1)
    own_terms = lax.dynamic_slice_in_dim(terms, section_index * slices_here, slices_here, axis=1)
    grad_band = place(own_terms, corner[0], extent, axis=2)
    from_below = from_behind(grad_band[:, :, :margin], "tile", -grid_side)
    from_above = from_behind(grad_band[:, :, margin + tile_width :], "tile", grid_side)
    grad_wide = place(grad_band[:, :, margin : margin + tile_width], corner[1], extent, axis=3)
    grad_wide = grad_wide.at[:, :, low:].add(place(from_below, corner_below[1], extent, axis=3))
    grad_wide = grad_wide.at[:, :, :high].add(place(from_above, corner_above[1], extent, axis=3))
    half = tile_width // 2
    reps = lax.axis_size("rep")
    rep_index = lax.axis_index("rep")

    def rows_of(block, which):
        return lax.dynamic_slice_in_dim(block, which * half, half, axis=2)

    def to_tile(block, shift, cross):
        pairs = []
        for tile in range(tile_count):
            if 0 <= tile + shift < tile_count:
                for rep in range(reps):
                    pairs.append((tile * reps + rep, (tile + shift) * reps + (reps - 1 - rep if cross else rep)))
        return lax.ppermute(block, ("tile", "rep"), pairs)

    left_strip = grad_wide[..., :margin]
    right_strip = grad_wide[..., margin + tile_width :]
    from_right = to_tile(rows_of(left_strip, rep_index), -1, False) + to_tile(
        rows_of(left_strip, 1 - rep_index), -1, True
    )
    from_left = to_tile(rows_of(right_strip, rep_index), 1, False) + to_tile(
        rows_of(right_strip, 1 - rep_index), 1, True
    )
    middle = grad_wide[..., margin : margin + tile_width]
    kept = rows_of(middle, rep_index)
    shares = kept + lax.ppermute(rows_of(middle, 1 - rep_index), "rep", [(0, 1), (1, 0)])
    shares = shares.at[..., low:].add(from_right * has_right)
    shares = shares.at[..., :high].add(from_left * has_left)
    return (shares[0][:, None], shares[1][:, None])

def solution(mesh):
    in_specs = (
        P("section", "tile", None, None),
        P("section", "tile", None, None),
        P(),
        P("tile", "rep", None, None),
        P("tile", "rep", None, None, None),
    )
    out_specs = (P("section", "tile", "rep", None), P("section", "tile", "rep", None))
    return jax.shard_map(shards, mesh=mesh, in_specs=in_specs, out_specs=out_specs, check_vma=False)
```

```python
import math

import jax
import jax.numpy as jnp
from jax import lax
from jax.sharding import PartitionSpec as P

HALO = 128


dead_time = 0.1
background = 0.1
loss_weight = 0.1
fresnel = 0.5
highest = lax.Precision.HIGHEST


def from_behind(value, axis, by):
    peers = lax.axis_size(axis)
    pairs = [(i, i + by) for i in range(peers) if 0 <= i + by < peers]
    return lax.ppermute(value, axis, pairs)


def left_product(matrix, frames):
    return jnp.einsum(
        "mk,bkn->bmn", matrix, frames, precision=highest, preferred_element_type=jnp.float32
    )


def right_product(frames, matrix):
    return jnp.einsum(
        "bmk,kn->bmn", frames, matrix, precision=highest, preferred_element_type=jnp.float32
    )


def sandwich(table_re, table_im, wave_re, wave_im):
    first_re = left_product(table_re, wave_re) - left_product(table_im, wave_im)
    first_im = left_product(table_re, wave_im) + left_product(table_im, wave_re)
    out_re = right_product(first_re, table_re) - right_product(first_im, table_im)
    out_im = right_product(first_re, table_im) + right_product(first_im, table_re)
    return (out_re, out_im)


def dft_tables(length):
    indices = jnp.arange(length, dtype=jnp.int32)
    product = indices[:, None] * indices[None, :] % length
    angles = product.astype(jnp.float32) * (2.0 * math.pi / length)
    cosine_table = jnp.cos(angles)
    sine_table = jnp.sin(angles)
    shifted = jnp.where(indices < length // 2, indices, indices - length).astype(jnp.float32)
    kernel = math.pi * fresnel * shifted * shifted / length

    def spread(weights):
        first_part = jnp.dot(cosine_table * weights[None, :], cosine_table, precision=highest)
        second_part = jnp.dot(sine_table * weights[None, :], sine_table, precision=highest)
        return (first_part + second_part) / length

    near_table = (spread(jnp.cos(kernel)), spread(jnp.sin(kernel)))
    norm_scale = 1.0 / math.sqrt(length)
    far_table = (cosine_table * norm_scale, -sine_table * norm_scale)
    return (near_table, far_table)


def block_tables(table_re, table_im):
    left = jnp.stack([jnp.stack([table_re, -table_im]), jnp.stack([table_im, table_re])])
    right = jnp.stack([jnp.stack([table_re, table_im]), jnp.stack([-table_im, table_re])])
    return (left, right)


def stacked_sandwich(pair, wave_re, wave_im):
    left, right = pair
    wave = jnp.stack([wave_re, wave_im])
    first = jnp.einsum("abmk,bkn->amn", left, wave, precision=lax.Precision.HIGH, preferred_element_type=jnp.float32)
    out = jnp.einsum("bmk,bakn->amn", first, right, precision=lax.Precision.HIGH, preferred_element_type=jnp.float32)
    return (out[0], out[1])


def place(block, offset, total, axis):
    reach = total - block.shape[axis]
    widths = [(0, 0)] * block.ndim
    widths[axis] = (reach, reach)
    return lax.dynamic_slice_in_dim(jnp.pad(block, widths), reach - offset, total, axis=axis)


def likelihood_seed(far_re, far_im, observed):
    intensity = far_re * far_re + far_im * far_im
    shifted_total = intensity + background
    denominator = 1.0 + dead_time * shifted_total
    model_rate = shifted_total / denominator
    slope_term = loss_weight * (1.0 - observed / model_rate) / (denominator * denominator)
    return (2.0 * slope_term * far_re, 2.0 * slope_term * far_im)


def shards(phase_shift, absorption, probe_wave, positions, counts):
    slices_here = phase_shift.shape[0]
    tile_width = phase_shift.shape[2]
    frame_width = probe_wave.shape[1]
    sections = lax.axis_size("section")
    tile_count = lax.axis_size("tile")
    grid_side = math.isqrt(tile_count)
    margin = HALO
    extent = tile_width + 2 * margin
    section_index = lax.axis_index("section")
    column = lax.axis_index("tile") % grid_side
    has_left = (column > 0).astype(jnp.float32)
    has_right = (column < grid_side - 1).astype(jnp.float32)
    own_block = jnp.stack([phase_shift[:, 0], absorption[:, 0]])

    low, high = tile_width - margin, margin
    slices_total = sections * slices_here
    corner = positions[0, 0, 0]
    corner_above = from_behind(corner, "tile", grid_side)
    corner_below = from_behind(corner, "tile", -grid_side)
    to_left = from_behind(own_block[:, :, :, low:], "tile", 1) * has_left
    to_right = from_behind(own_block[:, :, :, :high], "tile", -1) * has_right
    wide = jnp.concatenate([to_left, own_block, to_right], axis=3)
    band_down = lax.dynamic_slice_in_dim(wide[:, :, low:], corner_below[1], frame_width, axis=3)
    band_up = lax.dynamic_slice_in_dim(wide[:, :, :high], corner_above[1], frame_width, axis=3)
    above = from_behind(band_down, "tile", grid_side)
    below = from_behind(band_up, "tile", -grid_side)
    column_band = jnp.concatenate(
        [above, lax.dynamic_slice_in_dim(wide, corner[1], frame_width, axis=3), below], axis=2
    )
    window = lax.dynamic_slice_in_dim(column_band, corner[0], frame_width, axis=2)
    damping = jnp.exp(-window[1])
    own_objects = jnp.stack([damping * jnp.cos(window[0]), damping * jnp.sin(window[0])], axis=1)
    split = frame_width // 2
    upper_all = lax.all_gather(own_objects[:, :, :split], "section", axis=0, tiled=True)
    backward_ring = [(peer, (peer + sections - 1) % sections) for peer in range(sections)]
    relative = [own_objects[:, :, split:]]
    for step in range(1, sections):
        relative.append(lax.ppermute(relative[-1], "section", backward_ring))
    doubled = jnp.concatenate(relative + relative[:-1], axis=0)
    lower_all = lax.dynamic_slice_in_dim(
        doubled, (sections - section_index) % sections * slices_here, sections * slices_here, axis=0
    )
    all_objects = jnp.concatenate([upper_all, lower_all], axis=2)
    near_table, far_table = lax.optimization_barrier(dft_tables(frame_width))
    near_pair = block_tables(*near_table)
    far_pair = block_tables(*far_table)
    near_back = block_tables(near_table[0], -near_table[1])
    far_back = block_tables(far_table[0], -far_table[1])
    observed = counts[0, 0, 0].astype(jnp.float32)
    wave_re, wave_im = probe_wave[0], probe_wave[1]
    exits = []
    for slice_no in range(slices_total):
        object_re = all_objects[slice_no, 0]
        object_im = all_objects[slice_no, 1]
        exit_re = object_re * wave_re - object_im * wave_im
        exit_im = object_re * wave_im + object_im * wave_re
        exits.append((exit_re, exit_im))
        pair = near_pair if slice_no < slices_total - 1 else far_pair
        wave_re, wave_im = stacked_sandwich(pair, exit_re, exit_im)
    grad_re, grad_im = likelihood_seed(wave_re, wave_im, observed)
    terms = []
    for slice_no in reversed(range(slices_total)):
        pair = near_back if slice_no < slices_total - 1 else far_back
        back_re, back_im = stacked_sandwich(pair, grad_re, grad_im)
        exit_re, exit_im = exits[slice_no]
        phase_term = back_im * exit_re - back_re * exit_im
        absorb_term = -(back_re * exit_re + back_im * exit_im)
        terms.append(jnp.stack([phase_term, absorb_term]))
        if slice_no > 0:
            object_re = all_objects[slice_no, 0]
            object_im = all_objects[slice_no, 1]
            grad_re = object_re * back_re + object_im * back_im
            grad_im = object_re * back_im - object_im * back_re
    terms = jnp.stack(terms[::-1], axis=1)
    own_terms = lax.dynamic_slice_in_dim(terms, section_index * slices_here, slices_here, axis=1)
    grad_band = place(own_terms, corner[0], extent, axis=2)
    from_below = from_behind(grad_band[:, :, :margin], "tile", -grid_side)
    from_above = from_behind(grad_band[:, :, margin + tile_width :], "tile", grid_side)
    grad_wide = place(grad_band[:, :, margin : margin + tile_width], corner[1], extent, axis=3)
    grad_wide = grad_wide.at[:, :, low:].add(place(from_below, corner_below[1], extent, axis=3))
    grad_wide = grad_wide.at[:, :, :high].add(place(from_above, corner_above[1], extent, axis=3))
    half = tile_width // 2
    reps = lax.axis_size("rep")
    rep_index = lax.axis_index("rep")

    def rows_of(block, which):
        return lax.dynamic_slice_in_dim(block, which * half, half, axis=2)

    def to_tile(block, shift, cross):
        pairs = []
        for tile in range(tile_count):
            if 0 <= tile + shift < tile_count:
                for rep in range(reps):
                    pairs.append((tile * reps + rep, (tile + shift) * reps + (reps - 1 - rep if cross else rep)))
        return lax.ppermute(block, ("tile", "rep"), pairs)

    left_strip = grad_wide[..., :margin]
    right_strip = grad_wide[..., margin + tile_width :]
    from_right = to_tile(rows_of(left_strip, rep_index), -1, False) + to_tile(
        rows_of(left_strip, 1 - rep_index), -1, True
    )
    from_left = to_tile(rows_of(right_strip, rep_index), 1, False) + to_tile(
        rows_of(right_strip, 1 - rep_index), 1, True
    )
    middle = grad_wide[..., margin : margin + tile_width]
    kept = rows_of(middle, rep_index)
    shares = kept + lax.ppermute(rows_of(middle, 1 - rep_index), "rep", [(0, 1), (1, 0)])
    shares = shares.at[..., low:].add(from_right * has_right)
    shares = shares.at[..., :high].add(from_left * has_left)
    return (shares[0][:, None], shares[1][:, None])

def solution(mesh):
    in_specs = (
        P("section", "tile", None, None),
        P("section", "tile", None, None),
        P(),
        P("tile", "rep", None, None),
        P("tile", "rep", None, None, None),
    )
    out_specs = (P("section", "tile", "rep", None), P("section", "tile", "rep", None))
    return jax.shard_map(shards, mesh=mesh, in_specs=in_specs, out_specs=out_specs, check_vma=False)
```

```python
import math

import jax
import jax.numpy as jnp
from jax import lax
from jax.sharding import PartitionSpec as P

HALO = 128


dead_time = 0.1
background = 0.1
loss_weight = 0.1
fresnel = 0.5
highest = lax.Precision.HIGHEST


def from_behind(value, axis, by):
    peers = lax.axis_size(axis)
    pairs = [(i, i + by) for i in range(peers) if 0 <= i + by < peers]
    return lax.ppermute(value, axis, pairs)


def left_product(matrix, frames):
    return jnp.einsum(
        "mk,bkn->bmn", matrix, frames, precision=highest, preferred_element_type=jnp.float32
    )


def right_product(frames, matrix):
    return jnp.einsum(
        "bmk,kn->bmn", frames, matrix, precision=highest, preferred_element_type=jnp.float32
    )


def sandwich(table_re, table_im, wave_re, wave_im):
    first_re = left_product(table_re, wave_re) - left_product(table_im, wave_im)
    first_im = left_product(table_re, wave_im) + left_product(table_im, wave_re)
    out_re = right_product(first_re, table_re) - right_product(first_im, table_im)
    out_im = right_product(first_re, table_im) + right_product(first_im, table_re)
    return (out_re, out_im)


def dft_tables(length):
    indices = jnp.arange(length, dtype=jnp.int32)
    product = indices[:, None] * indices[None, :] % length
    angles = product.astype(jnp.float32) * (2.0 * math.pi / length)
    cosine_table = jnp.cos(angles)
    sine_table = jnp.sin(angles)
    shifted = jnp.where(indices < length // 2, indices, indices - length).astype(jnp.float32)
    kernel = math.pi * fresnel * shifted * shifted / length

    def spread(weights):
        first_part = jnp.dot(cosine_table * weights[None, :], cosine_table, precision=highest)
        second_part = jnp.dot(sine_table * weights[None, :], sine_table, precision=highest)
        return (first_part + second_part) / length

    near_table = (spread(jnp.cos(kernel)), spread(jnp.sin(kernel)))
    norm_scale = 1.0 / math.sqrt(length)
    far_table = (cosine_table * norm_scale, -sine_table * norm_scale)
    return (near_table, far_table)


def block_tables(table_re, table_im):
    left = jnp.stack([jnp.stack([table_re, -table_im]), jnp.stack([table_im, table_re])])
    right = jnp.stack([jnp.stack([table_re, table_im]), jnp.stack([-table_im, table_re])])
    return (left, right)


def stacked_sandwich(pair, wave_re, wave_im):
    left, right = pair
    wave = jnp.stack([wave_re, wave_im])
    first = jnp.einsum("abmk,bkn->amn", left, wave, precision=lax.Precision.HIGH, preferred_element_type=jnp.float32)
    out = jnp.einsum("bmk,bakn->amn", first, right, precision=lax.Precision.HIGH, preferred_element_type=jnp.float32)
    return (out[0], out[1])


def place(block, offset, total, axis):
    reach = total - block.shape[axis]
    widths = [(0, 0)] * block.ndim
    widths[axis] = (reach, reach)
    return lax.dynamic_slice_in_dim(jnp.pad(block, widths), reach - offset, total, axis=axis)


def likelihood_seed(far_re, far_im, observed):
    intensity = far_re * far_re + far_im * far_im
    shifted_total = intensity + background
    denominator = 1.0 + dead_time * shifted_total
    model_rate = shifted_total / denominator
    slope_term = loss_weight * (1.0 - observed / model_rate) / (denominator * denominator)
    return (2.0 * slope_term * far_re, 2.0 * slope_term * far_im)


def shards(phase_shift, absorption, probe_wave, positions, counts):
    slices_here = phase_shift.shape[0]
    tile_width = phase_shift.shape[2]
    frame_width = probe_wave.shape[1]
    sections = lax.axis_size("section")
    tile_count = lax.axis_size("tile")
    grid_side = math.isqrt(tile_count)
    margin = HALO
    extent = tile_width + 2 * margin
    section_index = lax.axis_index("section")
    column = lax.axis_index("tile") % grid_side
    has_left = (column > 0).astype(jnp.float32)
    has_right = (column < grid_side - 1).astype(jnp.float32)
    own_block = jnp.stack([phase_shift[:, 0], absorption[:, 0]])

    low, high = tile_width - margin, margin
    slices_total = sections * slices_here
    corner = positions[0, 0, 0]
    corner_above = from_behind(corner, "tile", grid_side)
    corner_below = from_behind(corner, "tile", -grid_side)
    to_left = from_behind(own_block[:, :, :, low:], "tile", 1) * has_left
    to_right = from_behind(own_block[:, :, :, :high], "tile", -1) * has_right
    wide = jnp.concatenate([to_left, own_block, to_right], axis=3)
    band_down = lax.dynamic_slice_in_dim(wide[:, :, low:], corner_below[1], frame_width, axis=3)
    band_up = lax.dynamic_slice_in_dim(wide[:, :, :high], corner_above[1], frame_width, axis=3)
    above = from_behind(band_down, "tile", grid_side)
    below = from_behind(band_up, "tile", -grid_side)
    column_band = jnp.concatenate(
        [above, lax.dynamic_slice_in_dim(wide, corner[1], frame_width, axis=3), below], axis=2
    )
    window = lax.dynamic_slice_in_dim(column_band, corner[0], frame_width, axis=2)
    damping = jnp.exp(-window[1])
    own_objects = jnp.stack([damping * jnp.cos(window[0]), damping * jnp.sin(window[0])], axis=1)
    split = frame_width // 2
    upper_all = lax.all_gather(own_objects[:, :, :split], "section", axis=0, tiled=True)
    relative = [own_objects[:, :, split:]]
    for shift in range(1, sections):
        pairs = [((peer + shift) % sections, peer) for peer in range(sections)]
        relative.append(lax.ppermute(relative[0], "section", pairs))
    doubled = jnp.concatenate(relative + relative[:-1], axis=0)
    lower_all = lax.dynamic_slice_in_dim(
        doubled, (sections - section_index) % sections * slices_here, sections * slices_here, axis=0
    )
    all_objects = jnp.concatenate([upper_all, lower_all], axis=2)
    near_table, far_table = lax.optimization_barrier(dft_tables(frame_width))
    near_pair = block_tables(*near_table)
    far_pair = block_tables(*far_table)
    near_back = block_tables(near_table[0], -near_table[1])
    far_back = block_tables(far_table[0], -far_table[1])
    observed = counts[0, 0, 0].astype(jnp.float32)
    wave_re, wave_im = probe_wave[0], probe_wave[1]
    exits = []
    for slice_no in range(slices_total):
        object_re = all_objects[slice_no, 0]
        object_im = all_objects[slice_no, 1]
        exit_re = object_re * wave_re - object_im * wave_im
        exit_im = object_re * wave_im + object_im * wave_re
        exits.append((exit_re, exit_im))
        pair = near_pair if slice_no < slices_total - 1 else far_pair
        wave_re, wave_im = stacked_sandwich(pair, exit_re, exit_im)
    grad_re, grad_im = likelihood_seed(wave_re, wave_im, observed)
    terms = []
    for slice_no in reversed(range(slices_total)):
        pair = near_back if slice_no < slices_total - 1 else far_back
        back_re, back_im = stacked_sandwich(pair, grad_re, grad_im)
        exit_re, exit_im = exits[slice_no]
        phase_term = back_im * exit_re - back_re * exit_im
        absorb_term = -(back_re * exit_re + back_im * exit_im)
        terms.append(jnp.stack([phase_term, absorb_term]))
        if slice_no > 0:
            object_re = all_objects[slice_no, 0]
            object_im = all_objects[slice_no, 1]
            grad_re = object_re * back_re + object_im * back_im
            grad_im = object_re * back_im - object_im * back_re
    terms = jnp.stack(terms[::-1], axis=1)
    own_terms = lax.dynamic_slice_in_dim(terms, section_index * slices_here, slices_here, axis=1)
    grad_band = place(own_terms, corner[0], extent, axis=2)
    from_below = from_behind(grad_band[:, :, :margin], "tile", -grid_side)
    from_above = from_behind(grad_band[:, :, margin + tile_width :], "tile", grid_side)
    grad_wide = place(grad_band[:, :, margin : margin + tile_width], corner[1], extent, axis=3)
    grad_wide = grad_wide.at[:, :, low:].add(place(from_below, corner_below[1], extent, axis=3))
    grad_wide = grad_wide.at[:, :, :high].add(place(from_above, corner_above[1], extent, axis=3))
    half = tile_width // 2
    reps = lax.axis_size("rep")
    rep_index = lax.axis_index("rep")

    def rows_of(block, which):
        return lax.dynamic_slice_in_dim(block, which * half, half, axis=2)

    def to_tile(block, shift, cross):
        pairs = []
        for tile in range(tile_count):
            if 0 <= tile + shift < tile_count:
                for rep in range(reps):
                    pairs.append((tile * reps + rep, (tile + shift) * reps + (reps - 1 - rep if cross else rep)))
        return lax.ppermute(block, ("tile", "rep"), pairs)

    left_strip = grad_wide[..., :margin]
    right_strip = grad_wide[..., margin + tile_width :]
    from_right = to_tile(rows_of(left_strip, rep_index), -1, False) + to_tile(
        rows_of(left_strip, 1 - rep_index), -1, True
    )
    from_left = to_tile(rows_of(right_strip, rep_index), 1, False) + to_tile(
        rows_of(right_strip, 1 - rep_index), 1, True
    )
    middle = grad_wide[..., margin : margin + tile_width]
    kept = rows_of(middle, rep_index)
    shares = kept + lax.ppermute(rows_of(middle, 1 - rep_index), "rep", [(0, 1), (1, 0)])
    shares = shares.at[..., low:].add(from_right * has_right)
    shares = shares.at[..., :high].add(from_left * has_left)
    return (shares[0][:, None], shares[1][:, None])

def solution(mesh):
    in_specs = (
        P("section", "tile", None, None),
        P("section", "tile", None, None),
        P(),
        P("tile", "rep", None, None),
        P("tile", "rep", None, None, None),
    )
    out_specs = (P("section", "tile", "rep", None), P("section", "tile", "rep", None))
    return jax.shard_map(shards, mesh=mesh, in_specs=in_specs, out_specs=out_specs, check_vma=False)
```

```python
import math

import jax
import jax.numpy as jnp
from jax import lax
from jax.sharding import PartitionSpec as P

HALO = 128


dead_time = 0.1
background = 0.1
loss_weight = 0.1
fresnel = 0.5
highest = lax.Precision.HIGHEST


def from_behind(value, axis, by):
    peers = lax.axis_size(axis)
    pairs = [(i, i + by) for i in range(peers) if 0 <= i + by < peers]
    return lax.ppermute(value, axis, pairs)


def left_product(matrix, frames):
    return jnp.einsum(
        "mk,bkn->bmn", matrix, frames, precision=highest, preferred_element_type=jnp.float32
    )


def right_product(frames, matrix):
    return jnp.einsum(
        "bmk,kn->bmn", frames, matrix, precision=highest, preferred_element_type=jnp.float32
    )


def sandwich(table_re, table_im, wave_re, wave_im):
    first_re = left_product(table_re, wave_re) - left_product(table_im, wave_im)
    first_im = left_product(table_re, wave_im) + left_product(table_im, wave_re)
    out_re = right_product(first_re, table_re) - right_product(first_im, table_im)
    out_im = right_product(first_re, table_im) + right_product(first_im, table_re)
    return (out_re, out_im)


def dft_tables(length):
    indices = jnp.arange(length, dtype=jnp.int32)
    product = indices[:, None] * indices[None, :] % length
    angles = product.astype(jnp.float32) * (2.0 * math.pi / length)
    cosine_table = jnp.cos(angles)
    sine_table = jnp.sin(angles)
    shifted = jnp.where(indices < length // 2, indices, indices - length).astype(jnp.float32)
    kernel = math.pi * fresnel * shifted * shifted / length

    def spread(weights):
        first_part = jnp.dot(cosine_table * weights[None, :], cosine_table, precision=highest)
        second_part = jnp.dot(sine_table * weights[None, :], sine_table, precision=highest)
        return (first_part + second_part) / length

    near_table = (spread(jnp.cos(kernel)), spread(jnp.sin(kernel)))
    norm_scale = 1.0 / math.sqrt(length)
    far_table = (cosine_table * norm_scale, -sine_table * norm_scale)
    return (near_table, far_table)


def block_tables(table_re, table_im):
    left = jnp.stack([jnp.stack([table_re, -table_im]), jnp.stack([table_im, table_re])])
    right = jnp.stack([jnp.stack([table_re, table_im]), jnp.stack([-table_im, table_re])])
    return (left, right)


def stacked_sandwich(pair, wave_re, wave_im):
    left, right = pair
    wave = jnp.stack([wave_re, wave_im])
    first = jnp.einsum("abmk,bkn->amn", left, wave, precision=lax.Precision.HIGH, preferred_element_type=jnp.float32)
    out = jnp.einsum("bmk,bakn->amn", first, right, precision=lax.Precision.HIGH, preferred_element_type=jnp.float32)
    return (out[0], out[1])


def place(block, offset, total, axis):
    reach = total - block.shape[axis]
    widths = [(0, 0)] * block.ndim
    widths[axis] = (reach, reach)
    return lax.dynamic_slice_in_dim(jnp.pad(block, widths), reach - offset, total, axis=axis)


def likelihood_seed(far_re, far_im, observed):
    intensity = far_re * far_re + far_im * far_im
    shifted_total = intensity + background
    denominator = 1.0 + dead_time * shifted_total
    model_rate = shifted_total / denominator
    slope_term = loss_weight * (1.0 - observed / model_rate) / (denominator * denominator)
    return (2.0 * slope_term * far_re, 2.0 * slope_term * far_im)


def shards(phase_shift, absorption, probe_wave, positions, counts):
    slices_here = phase_shift.shape[0]
    tile_width = phase_shift.shape[2]
    frame_width = probe_wave.shape[1]
    sections = lax.axis_size("section")
    tile_count = lax.axis_size("tile")
    grid_side = math.isqrt(tile_count)
    margin = HALO
    extent = tile_width + 2 * margin
    section_index = lax.axis_index("section")
    column = lax.axis_index("tile") % grid_side
    has_left = (column > 0).astype(jnp.float32)
    has_right = (column < grid_side - 1).astype(jnp.float32)
    own_block = jnp.stack([phase_shift[:, 0], absorption[:, 0]])

    low, high = tile_width - margin, margin
    slices_total = sections * slices_here
    corner = positions[0, 0, 0]
    corner_above = from_behind(corner, "tile", grid_side)
    corner_below = from_behind(corner, "tile", -grid_side)
    to_left = from_behind(own_block[:, :, :, low:], "tile", 1) * has_left
    to_right = from_behind(own_block[:, :, :, :high], "tile", -1) * has_right
    wide = jnp.concatenate([to_left, own_block, to_right], axis=3)
    band_down = lax.dynamic_slice_in_dim(wide[:, :, low:], corner_below[1], frame_width, axis=3)
    band_up = lax.dynamic_slice_in_dim(wide[:, :, :high], corner_above[1], frame_width, axis=3)
    above = from_behind(band_down, "tile", grid_side)
    below = from_behind(band_up, "tile", -grid_side)
    column_band = jnp.concatenate(
        [above, lax.dynamic_slice_in_dim(wide, corner[1], frame_width, axis=3), below], axis=2
    )
    window = lax.dynamic_slice_in_dim(column_band, corner[0], frame_width, axis=2)
    damping = jnp.exp(-window[1])
    own_objects = jnp.stack([damping * jnp.cos(window[0]), damping * jnp.sin(window[0])], axis=1)
    relative = [own_objects]
    for shift in range(1, sections):
        pairs = [((peer + shift) % sections, peer) for peer in range(sections)]
        relative.append(lax.ppermute(own_objects, "section", pairs))
    doubled = jnp.concatenate(relative + relative[:-1], axis=0)
    all_objects = lax.dynamic_slice_in_dim(
        doubled, (sections - section_index) % sections * slices_here, sections * slices_here, axis=0
    )
    near_table, far_table = lax.optimization_barrier(dft_tables(frame_width))
    near_pair = block_tables(*near_table)
    far_pair = block_tables(*far_table)
    near_back = block_tables(near_table[0], -near_table[1])
    far_back = block_tables(far_table[0], -far_table[1])
    observed = counts[0, 0, 0].astype(jnp.float32)
    wave_re, wave_im = probe_wave[0], probe_wave[1]
    exits = []
    for slice_no in range(slices_total):
        object_re = all_objects[slice_no, 0]
        object_im = all_objects[slice_no, 1]
        exit_re = object_re * wave_re - object_im * wave_im
        exit_im = object_re * wave_im + object_im * wave_re
        exits.append((exit_re, exit_im))
        pair = near_pair if slice_no < slices_total - 1 else far_pair
        wave_re, wave_im = stacked_sandwich(pair, exit_re, exit_im)
    grad_re, grad_im = likelihood_seed(wave_re, wave_im, observed)
    terms = []
    for slice_no in reversed(range(slices_total)):
        pair = near_back if slice_no < slices_total - 1 else far_back
        back_re, back_im = stacked_sandwich(pair, grad_re, grad_im)
        exit_re, exit_im = exits[slice_no]
        phase_term = back_im * exit_re - back_re * exit_im
        absorb_term = -(back_re * exit_re + back_im * exit_im)
        terms.append(jnp.stack([phase_term, absorb_term]))
        if slice_no > 0:
            object_re = all_objects[slice_no, 0]
            object_im = all_objects[slice_no, 1]
            grad_re = object_re * back_re + object_im * back_im
            grad_im = object_re * back_im - object_im * back_re
    terms = jnp.stack(terms[::-1], axis=1)
    own_terms = lax.dynamic_slice_in_dim(terms, section_index * slices_here, slices_here, axis=1)
    grad_band = place(own_terms, corner[0], extent, axis=2)
    from_below = from_behind(grad_band[:, :, :margin], "tile", -grid_side)
    from_above = from_behind(grad_band[:, :, margin + tile_width :], "tile", grid_side)
    grad_wide = place(grad_band[:, :, margin : margin + tile_width], corner[1], extent, axis=3)
    grad_wide = grad_wide.at[:, :, low:].add(place(from_below, corner_below[1], extent, axis=3))
    grad_wide = grad_wide.at[:, :, :high].add(place(from_above, corner_above[1], extent, axis=3))
    half = tile_width // 2
    reps = lax.axis_size("rep")
    rep_index = lax.axis_index("rep")

    def rows_of(block, which):
        return lax.dynamic_slice_in_dim(block, which * half, half, axis=2)

    def to_tile(block, shift, cross):
        pairs = []
        for tile in range(tile_count):
            if 0 <= tile + shift < tile_count:
                for rep in range(reps):
                    pairs.append((tile * reps + rep, (tile + shift) * reps + (reps - 1 - rep if cross else rep)))
        return lax.ppermute(block, ("tile", "rep"), pairs)

    left_strip = grad_wide[..., :margin]
    right_strip = grad_wide[..., margin + tile_width :]
    from_right = to_tile(rows_of(left_strip, rep_index), -1, False) + to_tile(
        rows_of(left_strip, 1 - rep_index), -1, True
    )
    from_left = to_tile(rows_of(right_strip, rep_index), 1, False) + to_tile(
        rows_of(right_strip, 1 - rep_index), 1, True
    )
    middle = grad_wide[..., margin : margin + tile_width]
    kept = rows_of(middle, rep_index)
    shares = kept + lax.ppermute(rows_of(middle, 1 - rep_index), "rep", [(0, 1), (1, 0)])
    shares = shares.at[..., low:].add(from_right * has_right)
    shares = shares.at[..., :high].add(from_left * has_left)
    return (shares[0][:, None], shares[1][:, None])

def solution(mesh):
    in_specs = (
        P("section", "tile", None, None),
        P("section", "tile", None, None),
        P(),
        P("tile", "rep", None, None),
        P("tile", "rep", None, None, None),
    )
    out_specs = (P("section", "tile", "rep", None), P("section", "tile", "rep", None))
    return jax.shard_map(shards, mesh=mesh, in_specs=in_specs, out_specs=out_specs, check_vma=False)
```

```python
import math

import jax
import jax.numpy as jnp
from jax import lax
from jax.sharding import PartitionSpec as P

HALO = 128


dead_time = 0.1
background = 0.1
loss_weight = 0.1
fresnel = 0.5
highest = lax.Precision.HIGHEST


def from_behind(value, axis, by):
    peers = lax.axis_size(axis)
    pairs = [(i, i + by) for i in range(peers) if 0 <= i + by < peers]
    return lax.ppermute(value, axis, pairs)


def left_product(matrix, frames):
    return jnp.einsum(
        "mk,bkn->bmn", matrix, frames, precision=highest, preferred_element_type=jnp.float32
    )


def right_product(frames, matrix):
    return jnp.einsum(
        "bmk,kn->bmn", frames, matrix, precision=highest, preferred_element_type=jnp.float32
    )


def sandwich(table_re, table_im, wave_re, wave_im):
    first_re = left_product(table_re, wave_re) - left_product(table_im, wave_im)
    first_im = left_product(table_re, wave_im) + left_product(table_im, wave_re)
    out_re = right_product(first_re, table_re) - right_product(first_im, table_im)
    out_im = right_product(first_re, table_im) + right_product(first_im, table_re)
    return (out_re, out_im)


def dft_tables(length):
    indices = jnp.arange(length, dtype=jnp.int32)
    product = indices[:, None] * indices[None, :] % length
    angles = product.astype(jnp.float32) * (2.0 * math.pi / length)
    cosine_table = jnp.cos(angles)
    sine_table = jnp.sin(angles)
    shifted = jnp.where(indices < length // 2, indices, indices - length).astype(jnp.float32)
    kernel = math.pi * fresnel * shifted * shifted / length

    def spread(weights):
        first_part = jnp.dot(cosine_table * weights[None, :], cosine_table, precision=highest)
        second_part = jnp.dot(sine_table * weights[None, :], sine_table, precision=highest)
        return (first_part + second_part) / length

    near_table = (spread(jnp.cos(kernel)), spread(jnp.sin(kernel)))
    norm_scale = 1.0 / math.sqrt(length)
    far_table = (cosine_table * norm_scale, -sine_table * norm_scale)
    return (near_table, far_table)


def block_tables(table_re, table_im):
    left = jnp.stack([jnp.stack([table_re, -table_im]), jnp.stack([table_im, table_re])])
    right = jnp.stack([jnp.stack([table_re, table_im]), jnp.stack([-table_im, table_re])])
    return (left, right)


def stacked_sandwich(pair, wave_re, wave_im):
    left, right = pair
    wave = jnp.stack([wave_re, wave_im])
    first = jnp.einsum("abmk,bkn->amn", left, wave, precision=lax.Precision.HIGH, preferred_element_type=jnp.float32)
    out = jnp.einsum("bmk,bakn->amn", first, right, precision=lax.Precision.HIGH, preferred_element_type=jnp.float32)
    return (out[0], out[1])


def place(block, offset, total, axis):
    reach = total - block.shape[axis]
    widths = [(0, 0)] * block.ndim
    widths[axis] = (reach, reach)
    return lax.dynamic_slice_in_dim(jnp.pad(block, widths), reach - offset, total, axis=axis)


def likelihood_seed(far_re, far_im, observed):
    intensity = far_re * far_re + far_im * far_im
    shifted_total = intensity + background
    denominator = 1.0 + dead_time * shifted_total
    model_rate = shifted_total / denominator
    slope_term = loss_weight * (1.0 - observed / model_rate) / (denominator * denominator)
    return (2.0 * slope_term * far_re, 2.0 * slope_term * far_im)


def shards(phase_shift, absorption, probe_wave, positions, counts):
    slices_here = phase_shift.shape[0]
    tile_width = phase_shift.shape[2]
    frame_width = probe_wave.shape[1]
    sections = lax.axis_size("section")
    tile_count = lax.axis_size("tile")
    grid_side = math.isqrt(tile_count)
    margin = HALO
    extent = tile_width + 2 * margin
    section_index = lax.axis_index("section")
    column = lax.axis_index("tile") % grid_side
    has_left = (column > 0).astype(jnp.float32)
    has_right = (column < grid_side - 1).astype(jnp.float32)
    own_block = jnp.stack([phase_shift[:, 0], absorption[:, 0]])

    low, high = tile_width - margin, margin
    slices_total = sections * slices_here
    corner = positions[0, 0, 0]
    corner_above = from_behind(corner, "tile", grid_side)
    corner_below = from_behind(corner, "tile", -grid_side)
    to_left = from_behind(own_block[:, :, :, low:], "tile", 1) * has_left
    to_right = from_behind(own_block[:, :, :, :high], "tile", -1) * has_right
    wide = jnp.concatenate([to_left, own_block, to_right], axis=3)
    band_down = lax.dynamic_slice_in_dim(wide[:, :, low:], corner_below[1], frame_width, axis=3)
    band_up = lax.dynamic_slice_in_dim(wide[:, :, :high], corner_above[1], frame_width, axis=3)
    above = from_behind(band_down, "tile", grid_side)
    below = from_behind(band_up, "tile", -grid_side)
    column_band = jnp.concatenate(
        [above, lax.dynamic_slice_in_dim(wide, corner[1], frame_width, axis=3), below], axis=2
    )
    window = lax.dynamic_slice_in_dim(column_band, corner[0], frame_width, axis=2)
    damping = jnp.exp(-window[1])
    own_objects = jnp.stack([damping * jnp.cos(window[0]), damping * jnp.sin(window[0])], axis=1)
    all_objects = lax.all_gather(own_objects, "section", axis=0, tiled=True)
    near_table, far_table = lax.optimization_barrier(dft_tables(frame_width))
    near_pair = block_tables(*near_table)
    far_pair = block_tables(*far_table)
    near_back = block_tables(near_table[0], -near_table[1])
    far_back = block_tables(far_table[0], -far_table[1])
    observed = counts[0, 0, 0].astype(jnp.float32)
    wave_re, wave_im = probe_wave[0], probe_wave[1]
    exits = []
    for slice_no in range(slices_total):
        object_re = all_objects[slice_no, 0]
        object_im = all_objects[slice_no, 1]
        exit_re = object_re * wave_re - object_im * wave_im
        exit_im = object_re * wave_im + object_im * wave_re
        exits.append((exit_re, exit_im))
        pair = near_pair if slice_no < slices_total - 1 else far_pair
        wave_re, wave_im = stacked_sandwich(pair, exit_re, exit_im)
    grad_re, grad_im = likelihood_seed(wave_re, wave_im, observed)
    terms = []
    for slice_no in reversed(range(slices_total)):
        pair = near_back if slice_no < slices_total - 1 else far_back
        back_re, back_im = stacked_sandwich(pair, grad_re, grad_im)
        exit_re, exit_im = exits[slice_no]
        phase_term = back_im * exit_re - back_re * exit_im
        absorb_term = -(back_re * exit_re + back_im * exit_im)
        terms.append(jnp.stack([phase_term, absorb_term]))
        if slice_no > 0:
            object_re = all_objects[slice_no, 0]
            object_im = all_objects[slice_no, 1]
            grad_re = object_re * back_re + object_im * back_im
            grad_im = object_re * back_im - object_im * back_re
    terms = jnp.stack(terms[::-1], axis=1)
    own_terms = lax.dynamic_slice_in_dim(terms, section_index * slices_here, slices_here, axis=1)
    grad_band = place(own_terms, corner[0], extent, axis=2)
    from_below = from_behind(grad_band[:, :, :margin], "tile", -grid_side)
    from_above = from_behind(grad_band[:, :, margin + tile_width :], "tile", grid_side)
    own_wide = place(grad_band[:, :, margin : margin + tile_width], corner[1], extent, axis=3)
    half = tile_width // 2
    rep_index = lax.axis_index("rep")
    early_sent = lax.dynamic_slice_in_dim(own_wide[..., margin : margin + tile_width], (1 - rep_index) * half, half, axis=2)
    early_swapped = lax.ppermute(early_sent, "rep", [(0, 1), (1, 0)])
    vert_wide = jnp.zeros_like(own_wide)
    vert_wide = vert_wide.at[:, :, low:].add(place(from_below, corner_below[1], extent, axis=3))
    vert_wide = vert_wide.at[:, :, :high].add(place(from_above, corner_above[1], extent, axis=3))
    grad_wide = own_wide + vert_wide
    half = tile_width // 2
    reps = lax.axis_size("rep")
    rep_index = lax.axis_index("rep")

    def rows_of(block, which):
        return lax.dynamic_slice_in_dim(block, which * half, half, axis=2)

    def to_tile(block, shift, cross):
        pairs = []
        for tile in range(tile_count):
            if 0 <= tile + shift < tile_count:
                for rep in range(reps):
                    pairs.append((tile * reps + rep, (tile + shift) * reps + (reps - 1 - rep if cross else rep)))
        return lax.ppermute(block, ("tile", "rep"), pairs)

    left_strip = grad_wide[..., :margin]
    right_strip = grad_wide[..., margin + tile_width :]
    from_right = to_tile(rows_of(left_strip, rep_index), -1, False) + to_tile(
        rows_of(left_strip, 1 - rep_index), -1, True
    )
    from_left = to_tile(rows_of(right_strip, rep_index), 1, False) + to_tile(
        rows_of(right_strip, 1 - rep_index), 1, True
    )
    middle = grad_wide[..., margin : margin + tile_width]
    vert_middle = vert_wide[..., margin : margin + tile_width]
    late_sent = lax.dynamic_slice_in_dim(vert_middle, (1 - rep_index) * low, margin, axis=2)
    late_swapped = lax.ppermute(late_sent, "rep", [(0, 1), (1, 0)])
    shares = rows_of(middle, rep_index) + early_swapped
    shares = lax.dynamic_update_slice_in_dim(
        shares,
        lax.dynamic_slice_in_dim(shares, rep_index * (half - margin), margin, axis=2) + late_swapped,
        rep_index * (half - margin),
        axis=2,
    )
    shares = shares.at[..., low:].add(from_right * has_right)
    shares = shares.at[..., :high].add(from_left * has_left)
    return (shares[0][:, None], shares[1][:, None])

def solution(mesh):
    in_specs = (
        P("section", "tile", None, None),
        P("section", "tile", None, None),
        P(),
        P("tile", "rep", None, None),
        P("tile", "rep", None, None, None),
    )
    out_specs = (P("section", "tile", "rep", None), P("section", "tile", "rep", None))
    return jax.shard_map(shards, mesh=mesh, in_specs=in_specs, out_specs=out_specs, check_vma=False)
```

```python
import math

import jax
import jax.numpy as jnp
from jax import lax
from jax.sharding import PartitionSpec as P

HALO = 128


dead_time = 0.1
background = 0.1
loss_weight = 0.1
fresnel = 0.5
highest = lax.Precision.HIGHEST


def from_behind(value, axis, by):
    peers = lax.axis_size(axis)
    pairs = [(i, i + by) for i in range(peers) if 0 <= i + by < peers]
    return lax.ppermute(value, axis, pairs)


def left_product(matrix, frames):
    return jnp.einsum(
        "mk,bkn->bmn", matrix, frames, precision=highest, preferred_element_type=jnp.float32
    )


def right_product(frames, matrix):
    return jnp.einsum(
        "bmk,kn->bmn", frames, matrix, precision=highest, preferred_element_type=jnp.float32
    )


def sandwich(table_re, table_im, wave_re, wave_im):
    first_re = left_product(table_re, wave_re) - left_product(table_im, wave_im)
    first_im = left_product(table_re, wave_im) + left_product(table_im, wave_re)
    out_re = right_product(first_re, table_re) - right_product(first_im, table_im)
    out_im = right_product(first_re, table_im) + right_product(first_im, table_re)
    return (out_re, out_im)


def dft_tables(length):
    indices = jnp.arange(length, dtype=jnp.int32)
    product = indices[:, None] * indices[None, :] % length
    angles = product.astype(jnp.float32) * (2.0 * math.pi / length)
    cosine_table = jnp.cos(angles)
    sine_table = jnp.sin(angles)
    shifted = jnp.where(indices < length // 2, indices, indices - length).astype(jnp.float32)
    kernel = math.pi * fresnel * shifted * shifted / length

    def spread(weights):
        first_part = jnp.dot(cosine_table * weights[None, :], cosine_table, precision=highest)
        second_part = jnp.dot(sine_table * weights[None, :], sine_table, precision=highest)
        return (first_part + second_part) / length

    near_table = (spread(jnp.cos(kernel)), spread(jnp.sin(kernel)))
    norm_scale = 1.0 / math.sqrt(length)
    far_table = (cosine_table * norm_scale, -sine_table * norm_scale)
    return (near_table, far_table)


def block_tables(table_re, table_im):
    left = jnp.stack([jnp.stack([table_re, -table_im]), jnp.stack([table_im, table_re])])
    right = jnp.stack([jnp.stack([table_re, table_im]), jnp.stack([-table_im, table_re])])
    return (left, right)


def stacked_sandwich(pair, wave_re, wave_im):
    left, right = pair
    wave = jnp.stack([wave_re, wave_im])
    first = jnp.einsum("abmk,bkn->amn", left, wave, precision=lax.Precision.HIGH, preferred_element_type=jnp.float32)
    out = jnp.einsum("bmk,bakn->amn", first, right, precision=lax.Precision.HIGH, preferred_element_type=jnp.float32)
    return (out[0], out[1])


def place(block, offset, total, axis):
    reach = total - block.shape[axis]
    widths = [(0, 0)] * block.ndim
    widths[axis] = (reach, reach)
    return lax.dynamic_slice_in_dim(jnp.pad(block, widths), reach - offset, total, axis=axis)


def likelihood_seed(far_re, far_im, observed):
    intensity = far_re * far_re + far_im * far_im
    shifted_total = intensity + background
    denominator = 1.0 + dead_time * shifted_total
    model_rate = shifted_total / denominator
    slope_term = loss_weight * (1.0 - observed / model_rate) / (denominator * denominator)
    return (2.0 * slope_term * far_re, 2.0 * slope_term * far_im)


def shards(phase_shift, absorption, probe_wave, positions, counts):
    slices_here = phase_shift.shape[0]
    tile_width = phase_shift.shape[2]
    frame_width = probe_wave.shape[1]
    sections = lax.axis_size("section")
    tile_count = lax.axis_size("tile")
    grid_side = math.isqrt(tile_count)
    margin = HALO
    extent = tile_width + 2 * margin
    section_index = lax.axis_index("section")
    column = lax.axis_index("tile") % grid_side
    has_left = (column > 0).astype(jnp.float32)
    has_right = (column < grid_side - 1).astype(jnp.float32)
    own_block = jnp.stack([phase_shift[:, 0], absorption[:, 0]])

    low, high = tile_width - margin, margin
    slices_total = sections * slices_here
    corner = positions[0, 0, 0]
    corner_above = from_behind(corner, "tile", grid_side)
    corner_below = from_behind(corner, "tile", -grid_side)
    to_left = from_behind(own_block[:, :, :, low:], "tile", 1) * has_left
    to_right = from_behind(own_block[:, :, :, :high], "tile", -1) * has_right
    wide = jnp.concatenate([to_left, own_block, to_right], axis=3)
    band_down = lax.dynamic_slice_in_dim(wide[:, :, low:], corner_below[1], frame_width, axis=3)
    band_up = lax.dynamic_slice_in_dim(wide[:, :, :high], corner_above[1], frame_width, axis=3)
    above = from_behind(band_down, "tile", grid_side)
    below = from_behind(band_up, "tile", -grid_side)
    column_band = jnp.concatenate(
        [above, lax.dynamic_slice_in_dim(wide, corner[1], frame_width, axis=3), below], axis=2
    )
    window = lax.dynamic_slice_in_dim(column_band, corner[0], frame_width, axis=2)
    damping = jnp.exp(-window[1])
    own_objects = jnp.stack([damping * jnp.cos(window[0]), damping * jnp.sin(window[0])], axis=1)
    all_objects = lax.all_gather(own_objects, "section", axis=0, tiled=True)
    near_table, far_table = lax.optimization_barrier(dft_tables(frame_width))
    near_pair = block_tables(*near_table)
    far_pair = block_tables(*far_table)
    near_back = block_tables(near_table[0], -near_table[1])
    far_back = block_tables(far_table[0], -far_table[1])
    observed = counts[0, 0, 0].astype(jnp.float32)
    wave_re, wave_im = probe_wave[0], probe_wave[1]
    exits = []
    for slice_no in range(slices_total):
        object_re = all_objects[slice_no, 0]
        object_im = all_objects[slice_no, 1]
        exit_re = object_re * wave_re - object_im * wave_im
        exit_im = object_re * wave_im + object_im * wave_re
        exits.append((exit_re, exit_im))
        pair = near_pair if slice_no < slices_total - 1 else far_pair
        wave_re, wave_im = stacked_sandwich(pair, exit_re, exit_im)
    grad_re, grad_im = likelihood_seed(wave_re, wave_im, observed)
    terms = []
    for slice_no in reversed(range(slices_total)):
        pair = near_back if slice_no < slices_total - 1 else far_back
        back_re, back_im = stacked_sandwich(pair, grad_re, grad_im)
        exit_re, exit_im = exits[slice_no]
        phase_term = back_im * exit_re - back_re * exit_im
        absorb_term = -(back_re * exit_re + back_im * exit_im)
        terms.append(jnp.stack([phase_term, absorb_term]))
        if slice_no > 0:
            object_re = all_objects[slice_no, 0]
            object_im = all_objects[slice_no, 1]
            grad_re = object_re * back_re + object_im * back_im
            grad_im = object_re * back_im - object_im * back_re
    terms = jnp.stack(terms[::-1], axis=1)
    own_terms = lax.dynamic_slice_in_dim(terms, section_index * slices_here, slices_here, axis=1)
    grad_band = place(own_terms, corner[0], extent, axis=2)
    from_below = from_behind(grad_band[:, :, :margin], "tile", -grid_side)
    from_above = from_behind(grad_band[:, :, margin + tile_width :], "tile", grid_side)
    own_wide = place(grad_band[:, :, margin : margin + tile_width], corner[1], extent, axis=3)
    half = tile_width // 2
    rep_index = lax.axis_index("rep")
    early_sent = lax.dynamic_slice_in_dim(own_wide[..., margin : margin + tile_width], (1 - rep_index) * half, half, axis=2)
    early_swapped = lax.ppermute(early_sent, "rep", [(0, 1), (1, 0)])
    vert_wide = jnp.zeros_like(own_wide)
    vert_wide = vert_wide.at[:, :, low:].add(place(from_below, corner_below[1], extent, axis=3))
    vert_wide = vert_wide.at[:, :, :high].add(place(from_above, corner_above[1], extent, axis=3))
    grad_wide = own_wide + vert_wide
    half = tile_width // 2
    reps = lax.axis_size("rep")
    rep_index = lax.axis_index("rep")

    def rows_of(block, which):
        return lax.dynamic_slice_in_dim(block, which * half, half, axis=2)

    def to_tile(block, shift, cross):
        pairs = []
        for tile in range(tile_count):
            if 0 <= tile + shift < tile_count:
                for rep in range(reps):
                    pairs.append((tile * reps + rep, (tile + shift) * reps + (reps - 1 - rep if cross else rep)))
        return lax.ppermute(block, ("tile", "rep"), pairs)

    def piece(block, which):
        return lax.dynamic_slice_in_dim(block, which * low, margin, axis=2)

    def routed(block, cut, shift):
        return to_tile(cut(block, rep_index), shift, False) + to_tile(cut(block, 1 - rep_index), shift, True)

    early_right = routed(own_wide[..., :margin], rows_of, -1)
    early_left = routed(own_wide[..., margin + tile_width :], rows_of, 1)
    late_right = routed(vert_wide[..., :margin], piece, -1)
    late_left = routed(vert_wide[..., margin + tile_width :], piece, 1)
    middle = grad_wide[..., margin : margin + tile_width]
    vert_middle = vert_wide[..., margin : margin + tile_width]
    late_sent = lax.dynamic_slice_in_dim(vert_middle, (1 - rep_index) * low, margin, axis=2)
    late_block = lax.ppermute(late_sent, "rep", [(0, 1), (1, 0)])
    late_block = late_block.at[..., low:].add(late_right * has_right)
    late_block = late_block.at[..., :high].add(late_left * has_left)
    shares = rows_of(middle, rep_index) + early_swapped
    shares = shares.at[..., low:].add(early_right * has_right)
    shares = shares.at[..., :high].add(early_left * has_left)
    offset = rep_index * (half - margin)
    shares = lax.dynamic_update_slice_in_dim(
        shares, lax.dynamic_slice_in_dim(shares, offset, margin, axis=2) + late_block, offset, axis=2
    )
    return (shares[0][:, None], shares[1][:, None])

def solution(mesh):
    in_specs = (
        P("section", "tile", None, None),
        P("section", "tile", None, None),
        P(),
        P("tile", "rep", None, None),
        P("tile", "rep", None, None, None),
    )
    out_specs = (P("section", "tile", "rep", None), P("section", "tile", "rep", None))
    return jax.shard_map(shards, mesh=mesh, in_specs=in_specs, out_specs=out_specs, check_vma=False)
```
